256 devices in a mesh: gx: 8 (over z), gy: 32 (over y, x, core).
Axes of the slice: x: 4, y: 4, z: 8, core: 2. Of those that a mesh axis runs over, the one named last changes fastest.
Arguments:
- leaf_maps: float32 [8, 32, 512, 512], P('gx', 'gy'), may hold values from -8 to 20, as said below
- leaf_fluxes: float32 [8, 32, 512, 128], P('gx', 'gy'), may hold values from -24 to 24
Outputs:
- boundary_values: float32 [8, 32, 512, 128], P('gx', 'gy')
The draws below stay inside these ranges and needn't reach their ends.
Inputs may be any that keep to these rules, and one draw needn't show every extreme that they name: `leaf_maps`: every leaf's map is symmetric and positive definite with smallest eigenvalue 0.1 or more.
All inputs are finite; a program needn't handle non-finite values.
Results may differ from the reference program's by a relative error of at most 0.0003.
Values sent between devices are 32-bit elements; how exact they have to be, the bound alone decides.
No kernel may reach another device: no remote copies, remote signals or barrier semaphores. Data moves between devices by JAX's collectives and lax.ppermute only.
A program may use at most 128 MiB of HBM per device.

```python
import math
from functools import partial
import jax
import jax.numpy as jnp
from jax import lax

PATCH = 128
SOURCES = 128
LEVELS = 4
PCOLS = 8
PROWS = 32


def draw_leaf_maps(key, part):
    points = 4 * PATCH
    first_key, second_key, third_key = jax.random.split(key, 3)
    shape_all = (PCOLS, PROWS, points, points)
    mixing = jax.random.normal(first_key, shape_all, jnp.float32)
    diagonal_part = jnp.exp(jax.random.uniform(second_key, (PCOLS, PROWS, points), jnp.float32, math.log(0.3), math.log(1.0)))
    bond_weights = jax.random.uniform(third_key, (PCOLS, PROWS, points), jnp.float32, 1.0, 4.0)
    mixed_part = jnp.einsum('abij,abkj->abik', mixing, mixing) / points
    point_index = jnp.arange(points)
    inside_edge = (point_index % PATCH != PATCH - 1).astype(jnp.float32)
    bond_weights = bond_weights * inside_edge
    previous = jnp.concatenate([jnp.zeros_like(bond_weights[..., :1]), bond_weights[..., :-1]], axis=-1)
    upper_shift = (point_index[:, None] + 1 == point_index[None, :]).astype(jnp.float32)
    coupling = bond_weights[..., :, None] * upper_shift
    laplace = -coupling - jnp.swapaxes(coupling, -1, -2)
    eye_matrix = jnp.eye(points, dtype=jnp.float32)
    return mixed_part + laplace + (diagonal_part + bond_weights + previous)[..., :, None] * eye_matrix


def shard_levels(key, shape, cuts, low, top_value):
    def one(dim, blocks):
        heights = jax.random.uniform(jax.random.fold_in(jax.random.fold_in(key, 6), dim), (blocks,), jnp.float32, low / len(cuts), top_value / len(cuts))
        return jnp.repeat(jnp.exp(heights), shape[dim] // blocks).reshape((-1,) + (1,) * (len(shape) - dim - 1))

    factor_of = one(*cuts[0])
    for cut in cuts[1:]:
        factor_of = factor_of * one(*cut)
    return factor_of


def noise(key, extent, spread, limit, cuts=(), kind=jnp.bfloat16):
    entries = spread * jax.random.normal(key, extent, jnp.float32)
    if cuts:
        entries = entries * shard_levels(key, extent, cuts, -0.22, 0.18)
    return jnp.clip(entries, -limit, limit).astype(kind)


def setup_inputs(seed: int = 0) -> dict:
    arg_keys = jax.random.split(jax.random.key(seed), 3)
    return {
        "leaf_maps": draw_leaf_maps(jax.random.fold_in(arg_keys[2], 71), 0),
        "leaf_fluxes": noise(arg_keys[1], (PCOLS, PROWS, 4 * PATCH, SOURCES), 4.0, 24.0, ((0, 8), (1, 32)), jnp.float32),
    }


side_names = ('left', 'right', 'bottom', 'top')

def side_spans(cols_count, rows_count, patch_side):
    lengths = {'left': rows_count * patch_side, 'right': rows_count * patch_side, 'bottom': cols_count * patch_side, 'top': cols_count * patch_side}
    starts = {}
    running = 0
    for side_name in side_names:
        starts[side_name] = running
        running = running + lengths[side_name]
    return (starts, lengths)

def merge_layout(direction):
    if direction == 'y':
        return (('top', 'bottom'), ((0, 'left'), (1, 'left'), (0, 'right'), (1, 'right'), (0, 'bottom'), (1, 'top')))
    return (('right', 'left'), ((0, 'left'), (1, 'right'), (0, 'bottom'), (1, 'bottom'), (0, 'top'), (1, 'top')))

def level_plan(levels):
    merge_plan = []
    cols_count, rows_count = (1, 1)
    for tree_level in range(levels):
        if tree_level % 2 == 0:
            merge_plan.append(('y', cols_count, rows_count))
            rows_count = rows_count * 2
        else:
            merge_plan.append(('x', cols_count, rows_count))
            cols_count = cols_count * 2
    return merge_plan

def take_rows(matrix, starts, lengths, side_name):
    return matrix[starts[side_name]:starts[side_name] + lengths[side_name]]

def take_block(matrix, starts, lengths, row_side, col_side):
    rows_part = take_rows(matrix, starts, lengths, row_side)
    return rows_part[:, starts[col_side]:starts[col_side] + lengths[col_side]]

def product(left_part, right_part):
    return jnp.dot(left_part, right_part, precision=lax.Precision.HIGHEST)

def solve_with(factor, rhs_part):
    halfway = jax.scipy.linalg.solve_triangular(factor, rhs_part, lower=True)
    return jax.scipy.linalg.solve_triangular(factor, halfway, lower=True, trans=1)

def diagonal_rows(matrix, starts, lengths, child_index, row_side, pieces):
    blocks = []
    for other_index, col_side in pieces:
        if other_index == child_index:
            blocks.append(take_block(matrix, starts, lengths, row_side, col_side))
        else:
            blocks.append(jnp.zeros((lengths[row_side], lengths[col_side]), matrix.dtype))
    return jnp.concatenate(blocks, axis=1)

def merge_pair(maps_pair, fluxes_pair, direction, cols_count, rows_count, patch_side):
    starts, lengths = side_spans(cols_count, rows_count, patch_side)
    face_sides, pieces = merge_layout(direction)
    interface_matrix = take_block(maps_pair[0], starts, lengths, face_sides[0], face_sides[0]) + take_block(maps_pair[1], starts, lengths, face_sides[1], face_sides[1])
    factor = jnp.linalg.cholesky(interface_matrix)
    across = jnp.concatenate([take_block(maps_pair[child_index], starts, lengths, face_sides[child_index], side_name) for child_index, side_name in pieces], axis=1)
    inward = jnp.concatenate([take_block(maps_pair[child_index], starts, lengths, side_name, face_sides[child_index]) for child_index, side_name in pieces], axis=0)
    face_flux = take_rows(fluxes_pair[0], starts, lengths, face_sides[0]) + take_rows(fluxes_pair[1], starts, lengths, face_sides[1])
    solved = solve_with(factor, across)
    weights = solve_with(factor, face_flux)
    assembled = jnp.concatenate([diagonal_rows(maps_pair[child_index], starts, lengths, child_index, side_name, pieces) for child_index, side_name in pieces], axis=0)
    merged_map = assembled - product(inward, solved)
    outer_flux = jnp.concatenate([take_rows(fluxes_pair[child_index], starts, lengths, side_name) for child_index, side_name in pieces], axis=0)
    merged_flux = outer_flux - product(inward, weights)
    return (merged_map, merged_flux, solved, weights)

def merge_vector(lower_map, upper_map, lower_flux, upper_flux, direction, cols_count, rows_count, patch_side):
    return merge_pair((lower_map, upper_map), (lower_flux, upper_flux), direction, cols_count, rows_count, patch_side)

def top_vector(lower_map, upper_map, lower_flux, upper_flux, direction, cols_count, rows_count, patch_side):
    starts, lengths = side_spans(cols_count, rows_count, patch_side)
    face_sides, pieces = merge_layout(direction)
    interface_matrix = take_block(lower_map, starts, lengths, face_sides[0], face_sides[0]) + take_block(upper_map, starts, lengths, face_sides[1], face_sides[1])
    factor = jnp.linalg.cholesky(interface_matrix)
    face_flux = take_rows(lower_flux, starts, lengths, face_sides[0]) + take_rows(upper_flux, starts, lengths, face_sides[1])
    return solve_with(factor, face_flux)

def merged_length(direction, cols_count, rows_count, patch_side):
    starts, lengths = side_spans(cols_count, rows_count, patch_side)
    face_sides, pieces = merge_layout(direction)
    return sum((lengths[side_name] for child_index, side_name in pieces))

def child_values(group_values, face_values, direction, cols_count, rows_count, patch_side, child_index):
    starts, lengths = side_spans(cols_count, rows_count, patch_side)
    face_sides, pieces = merge_layout(direction)
    offsets = {}
    running = 0
    for each_piece in pieces:
        offsets[each_piece] = running
        running = running + lengths[each_piece[1]]
    parts_list = []
    for side_name in side_names:
        if side_name == face_sides[child_index]:
            parts_list.append(face_values)
        else:
            first_row = offsets[child_index, side_name]
            parts_list.append(group_values[first_row:first_row + lengths[side_name]])
    return jnp.concatenate(parts_list, axis=0)

def pair_split(stacked_array, direction):
    if direction == 'y':
        return (stacked_array[:, 0::2], stacked_array[:, 1::2])
    return (stacked_array[0::2], stacked_array[1::2])

def pair_join(lower_part, upper_part, direction):
    if direction == 'y':
        joined = jnp.stack([lower_part, upper_part], axis=2)
        return joined.reshape((joined.shape[0], joined.shape[1] * 2) + joined.shape[3:])
    joined = jnp.stack([lower_part, upper_part], axis=1)
    return joined.reshape((joined.shape[0] * 2,) + joined.shape[2:])

def over_groups(function):
    return jax.vmap(jax.vmap(function))

def reference(leaf_maps, leaf_fluxes):
    patch_side = leaf_maps.shape[2] // 4
    merge_plan = level_plan(LEVELS)
    level_maps, fluxes = (leaf_maps, leaf_fluxes)
    stored = []
    top_weights = None
    for tree_level in range(LEVELS):
        direction, cols_count, rows_count = merge_plan[tree_level]
        lower_maps, upper_maps = pair_split(level_maps, direction)
        lower_fluxes, upper_fluxes = pair_split(fluxes, direction)
        if tree_level < LEVELS - 1:
            merger = partial(merge_vector, direction=direction, cols_count=cols_count, rows_count=rows_count, patch_side=patch_side)
            level_maps, fluxes, solved, weights = over_groups(merger)(lower_maps, upper_maps, lower_fluxes, upper_fluxes)
            stored.append((solved, weights))
        else:
            top_solver = partial(top_vector, direction=direction, cols_count=cols_count, rows_count=rows_count, patch_side=patch_side)
            top_weights = over_groups(top_solver)(lower_maps, upper_maps, lower_fluxes, upper_fluxes)
    direction, cols_count, rows_count = merge_plan[LEVELS - 1]
    face_values = -top_weights
    group_length = merged_length(direction, cols_count, rows_count, patch_side)
    group_values = jnp.zeros(face_values.shape[:2] + (group_length, face_values.shape[3]), face_values.dtype)
    for tree_level in range(LEVELS - 1, -1, -1):
        direction, cols_count, rows_count = merge_plan[tree_level]
        if tree_level < LEVELS - 1:
            solved, weights = stored[tree_level]
            face_values = -(over_groups(product)(solved, group_values) + weights)
        lower_values = over_groups(partial(child_values, direction=direction, cols_count=cols_count, rows_count=rows_count, patch_side=patch_side, child_index=0))(group_values, face_values)
        upper_values = over_groups(partial(child_values, direction=direction, cols_count=cols_count, rows_count=rows_count, patch_side=patch_side, child_index=1))(group_values, face_values)
        group_values = pair_join(lower_values, upper_values, direction)
    return group_values
```

```python
import jax
import jax.numpy as jnp
from jax import lax
from jax.experimental import pallas as pl
from jax.experimental.pallas import tpu as pltpu
from jax.sharding import PartitionSpec as P

N = 128
F32 = jnp.float32
HIGH = lax.Precision.HIGHEST

TILES1 = (
    (0, 0), (1, 0), (1, 1), (0, -1),
    (1, -1), (2, 0), (2, 1), (3, 0), (3, 1), (4, 0), (4, 1), (4, -1),
    (2, 2), (3, 2), (3, 3), (4, 2), (4, 3), (4, 4), (2, -1), (3, -1),
)
TILES2 = (
    (0, 0), (1, 0), (1, 1), (0, -1),
    (1, -1), (2, 0), (2, 1), (3, 0), (3, 1), (2, 2), (3, 2), (3, 3), (2, -1), (3, -1),
)
TILES3 = (
    (0, 0), (1, 0), (2, 0), (3, 0), (1, 1), (2, 1), (3, 1), (2, 2), (3, 2), (3, 3),
    (0, -1), (1, -1), (2, -1), (3, -1),
)
AT1 = {t: i for i, t in enumerate(TILES1)}
AT2 = {t: i for i, t in enumerate(TILES2)}
AT3 = {t: i for i, t in enumerate(TILES3)}
FIRST = 4


def roles():
    col = lax.axis_index("gx")
    row = lax.axis_index("gy")
    return col & 1, (col >> 1) & 1, row & 1, (row >> 1) & 1


def mm(x, y):
    return lax.dot_general(x, y, (((1,), (0,)), ((), ())), precision=HIGH, preferred_element_type=F32)


def mm_nt(x, y):
    return lax.dot_general(x, y, (((1,), (1,)), ((), ())), precision=HIGH, preferred_element_type=F32)


def mm_tn(x, y):
    return lax.dot_general(x, y, (((0,), (0,)), ((), ())), precision=HIGH, preferred_element_type=F32)


def over(x, rows=8):
    return jnp.broadcast_to(x, (rows, N))


def invert(x_ref):
    lane = lax.broadcasted_iota(jnp.int32, (8, N), 1)
    sub = lax.broadcasted_iota(jnp.int32, (8, N), 0)
    for j in range(N // 8):
        top = x_ref[8 * j : 8 * j + 8, :]
        cols = [over(top[:, 8 * j + c : 8 * j + c + 1]) for c in range(8)]
        for k in range(8):
            here = sub == k
            recip = 1.0 / over(cols[k][k : k + 1, :])
            fresh = []
            for c in range(8):
                if c == k:
                    fresh.append(jnp.where(here, recip, -cols[k] * recip))
                else:
                    scaled = over(cols[c][k : k + 1, :]) * recip
                    fresh.append(jnp.where(here, scaled, cols[c] - cols[k] * scaled))
            cols = fresh
        inside = (lane >= 8 * j) & (lane < 8 * j + 8)
        seed = jnp.where(inside, jnp.where(lane - 8 * j == sub, 1.0, 0.0), top)
        panel = cols[0] * over(seed[0:1, :])
        for c in range(1, 8):
            panel = panel + cols[c] * over(seed[c : c + 1, :])
        lines = [over(panel[k : k + 1, :]) for k in range(8)]
        for i in range(N // 8):
            if i == j:
                continue
            old = x_ref[8 * i : 8 * i + 8, :]
            new = jnp.where(inside, 0.0, old)
            for k in range(8):
                new = new - over(old[:, 8 * j + k : 8 * j + k + 1]) * lines[k]
            x_ref[8 * i : 8 * i + 8, :] = new
        x_ref[8 * j : 8 * j + 8, :] = panel


def merge0(own_map, own_flux, mate_map, mate_flux, kept, first, rest, y_ref, w_ref, x_ref, rhs, rows):
    a0, a1, b0, b1 = roles()
    core = b0
    mine_low = b0 == 0
    f1, h = 1 - a0, a0

    def at(side):
        return pl.ds(side * N, N) if isinstance(side, int) else pl.ds(pl.multiple_of(side * N, N), N)

    def entry(leaf, r, c):
        mine, mate = own_map[at(r), at(c)], mate_map[at(r), at(c)]
        return jnp.where(mine_low, mine, mate) if leaf == 0 else jnp.where(mine_low, mate, mine)

    def flux(leaf, r):
        mine, mate = own_flux[at(r), :], mate_flux[at(r), :]
        return jnp.where(mine_low, mine, mate) if leaf == 0 else jnp.where(mine_low, mate, mine)

    face, other = (3, 2), (2, 3)
    g_up = b1 == 0
    x_ref[...] = entry(0, 3, 3) + entry(1, 2, 2)
    owner = (0, 1, 0, 1)
    side = (f1, f1, h, h)
    for p in range(4):
        rhs[:, p * N : (p + 1) * N] = entry(owner[p], face[owner[p]], side[p])
        rows[p * N : (p + 1) * N, :] = entry(owner[p], side[p], face[owner[p]])
    rhs[:, 4 * N : 5 * N] = jnp.where(g_up, entry(1, 2, 3), entry(0, 3, 2))
    rows[4 * N : 5 * N, :] = jnp.where(g_up, entry(1, 3, 2), entry(0, 2, 3))
    rhs[:, 5 * N : 6 * N] = flux(0, 3) + flux(1, 2)
    invert(x_ref)
    out = mm(x_ref[...], rhs[...])
    y_ref[...] = out[:, : 5 * N]
    w_ref[...] = out[:, 5 * N :]
    for q in (0, 1, 2, 3, 4, -1):
        picked = [t for t in TILES1 if t[1] == q]
        for p, _ in picked:
            pass
        low = max(q, 0)
        cq = 5 if q < 0 else q
        sub = mm(rows[low * N : 5 * N, :], out[:, cq * N : (cq + 1) * N])
        for p in range(low, 5):
            value = -sub[(p - low) * N : (p - low + 1) * N, :]
            if q < 0:
                if p < 4:
                    value = value + flux(owner[p], side[p])
                else:
                    value = value + jnp.where(g_up, flux(1, 3), flux(0, 2))
            elif p < 4:
                if owner[p] == owner[q]:
                    value = value + entry(owner[p], side[p], side[q])
            elif q < 4:
                part = entry(1, 3, side[q]) if owner[q] == 1 else entry(0, 2, side[q])
                value = value + jnp.where(g_up if owner[q] == 1 else b1 == 1, part, 0.0)
            else:
                value = value + jnp.where(g_up, entry(1, 3, 3), entry(0, 2, 2))
            kept[AT1[(p, q)]] = value
    half = FIRST // 2
    for i in range(half):
        first[i] = kept[core * half + i]
    half = (len(TILES1) - FIRST) // 2
    for i in range(half):
        rest[i] = kept[FIRST + core * half + i]


def received(core, direct, swapped, index, half):
    where = core == index // half
    return jnp.where(where, direct[index % half], swapped[index % half])


def invert_pair(own, got, swapped, x_out, scratch, cross):
    _, _, core, _ = roles()

    def total(i):
        return own[i] + received(core, got, swapped, i, FIRST // 2)

    scratch[0] = total(0)
    cross[...] = total(1)
    scratch[1] = total(2)

    def step(i, carry):
        invert(scratch.at[i])

        @pl.when(i == 0)
        def _():
            t = mm(cross[...], scratch[0])
            scratch[1] = scratch[1] - mm_nt(t, cross[...])
            cross[...] = t

        return carry

    lax.fori_loop(0, 2, step, 0)
    t, x22 = cross[...], scratch[1]
    low = mm(x22, t)
    x_out[N:, N:] = x22
    x_out[N:, :N] = -low
    x_out[:N, N:] = -mm_tn(t, x22)
    x_out[:N, :N] = scratch[0] + mm_tn(t, low)


def merge1(x, own, got0, swp0, got1, swp1, kept, first, rest, a_ref, f_ref):
    a0, a1, core, b1 = roles()
    left = a0 == 0
    h_right = a1 == 0
    half0, half1 = FIRST // 2, (len(TILES1) - FIRST) // 2

    def mate(t):
        i = AT1[t]
        if i < FIRST:
            return received(core, got0, swp0, i, half0)
        return received(core, got1, swp1, i - FIRST, half1)

    mine_h = (a0 ^ a1) == 1

    def of_h(t):
        return jnp.where(mine_h, own[AT1[t]], mate(t))

    def of(which, t):
        return jnp.where(left if which == 0 else a0 == 1, own[AT1[t]], mate(t))

    for q in range(2):
        cols = slice(q * N, (q + 1) * N)
        a_ref[0:N, cols] = of(0, (4, q))
        a_ref[N : 2 * N, cols] = of(1, (4, q))
        a_ref[2 * N : 3 * N, cols] = of_h((2, q))
        a_ref[3 * N : 4 * N, cols] = of_h((3, q))
        f_ref[cols, :] = own[AT1[(q, -1)]] + mate((q, -1))
    yt = mm(a_ref[...], x[...])
    for q in (0, 1, 2, 3, -1):
        low = max(q, 0)
        if q < 0:
            sub = mm(yt, f_ref[...])
        else:
            sub = mm_nt(yt[low * N :], a_ref[q * N : (q + 1) * N, :])
        for p in range(low, 4):
            value = -sub[(p - low) * N : (p - low + 1) * N, :]
            if q < 0:
                value = value + (of(p, (4, -1)) if p < 2 else of_h((p, -1)))
            elif p >= 2 and q >= 2:
                value = value + of_h((p, q))
            elif p >= 2:
                holds = h_right if q == 1 else a1 == 1
                value = value + jnp.where(holds, of_h((4, p)).T, 0.0)
            elif p == q:
                value = value + of(p, (4, 4))
            kept[AT2[(p, q)]] = value
    half = FIRST // 2
    for i in range(half):
        first[i] = kept[core * half + i]
    half = (len(TILES2) - FIRST) // 2
    for i in range(half):
        rest[i] = kept[FIRST + core * half + i]


def merge2(x, own, got0, swp0, got1, swp1, kept, send, a_ref, f_ref):
    _, _, core, b1 = roles()
    low_mine = b1 == 0
    half0, half1 = FIRST // 2, (len(TILES2) - FIRST) // 2

    def mate(t):
        i = AT2[t]
        if i < FIRST:
            return received(core, got0, swp0, i, half0)
        return received(core, got1, swp1, i - FIRST, half1)

    def of(which, t):
        return jnp.where(low_mine if which == 0 else b1 == 1, own[AT2[t]], mate(t))

    for q in range(2):
        cols = slice(q * N, (q + 1) * N)
        for p in range(4):
            a_ref[p * N : (p + 1) * N, cols] = of(p // 2, (2 + p % 2, q))
        f_ref[cols, :] = own[AT2[(q, -1)]] + mate((q, -1))
    yt = mm(a_ref[...], x[...])
    for q in (0, 1, 2, 3, -1):
        low = max(q, 0)
        if q < 0:
            sub = mm(yt, f_ref[...])
        else:
            sub = mm_nt(yt[low * N :], a_ref[q * N : (q + 1) * N, :])
        for p in range(low, 4):
            value = -sub[(p - low) * N : (p - low + 1) * N, :]
            if q < 0:
                value = value + of(p // 2, (2 + p % 2, -1))
            elif p // 2 == q // 2:
                value = value + of(p // 2, (2 + p % 2, 2 + q % 2))
            kept[AT3[(p, q)]] = value
    half = len(TILES3) // 2
    for i in range(half):
        send[i] = kept[core * half + i]


def solve3(own, got, swapped, u_out, send, s, x):
    _, _, core, _ = roles()
    half = len(TILES3) // 2
    for i in range(len(TILES3)):
        s[i] = own[i] + received(core, got, swapped, i, half)

    def step(j, carry):
        x[...] = s[j * 4 - (j * (j - 1)) // 2]
        invert(x)
        s[j * 4 - (j * (j - 1)) // 2] = x[...]
        for k in range(3):

            @pl.when(j == k)
            def _(k=k):
                lows = [mm(s[AT3[(i, k)]], x[...]) for i in range(k + 1, 4)]
                for i in range(k + 1, 4):
                    for m in range(k + 1, i + 1):
                        s[AT3[(i, m)]] = s[AT3[(i, m)]] - mm_nt(lows[i - k - 1], s[AT3[(m, k)]])
                    s[AT3[(i, -1)]] = s[AT3[(i, -1)]] - mm(lows[i - k - 1], s[AT3[(k, -1)]])
                for i in range(k + 1, 4):
                    s[AT3[(i, k)]] = lows[i - k - 1]

        return carry

    lax.fori_loop(0, 4, step, 0)
    w = [None] * 4
    for k in (3, 2, 1, 0):
        w[k] = mm(s[AT3[(k, k)]], s[AT3[(k, -1)]])
        for i in range(k + 1, 4):
            w[k] = w[k] - mm_tn(s[AT3[(i, k)]], w[i])
        u_out[k] = -w[k]
    for i in range(2):
        send[i] = u_out[2 * core + i]


def descend(u_own, got, swapped, x2, a2, f2, x1, a1_ref, f1, y0, w0, out, u, v):
    a0, a1, b0, b1 = roles()
    inner = (a0 ^ a1) == 1
    for i in range(4):
        u[i * N : (i + 1) * N, :] = jnp.where(inner, u_own[i], received(b0, got, swapped, i, 2))
    face2 = -mm(x2[...], mm_tn(a2[...], u[...]) + f2[...])
    v[: 2 * N, :] = face2
    v[2 * N :, :] = jnp.where(b1 == 0, u[: 2 * N, :], u[2 * N :, :])
    face1 = -mm(x1[...], mm_tn(a1_ref[...], v[...]) + f1[...])
    side_h = jnp.where(inner, v[2 * N :, :], 0.0)
    side_g = jnp.where(a0 == 0, face2[:N, :], face2[N:, :])
    face0 = mm(y0[:, : 2 * N], face1) + mm(y0[:, 2 * N : 4 * N], side_h) + mm(y0[:, 4 * N :], side_g) + w0[...]
    mine_1 = jnp.where(b0 == 0, face1[:N, :], face1[N:, :])
    mine_h = jnp.where(b0 == 0, side_h[:N, :], side_h[N:, :])
    mine_g = jnp.where((b0 ^ b1) == 1, side_g, 0.0)
    out[:N, :] = jnp.where(a0 == 0, mine_h, mine_1)
    out[N : 2 * N, :] = jnp.where(a0 == 0, mine_1, mine_h)
    out[2 * N : 3 * N, :] = jnp.where(b0 == 0, mine_g, -face0)
    out[3 * N :, :] = jnp.where(b0 == 0, -face0, mine_g)


def call(body, name, outs, scratch, *args):
    vmem = pl.BlockSpec(memory_space=pltpu.VMEM)
    return pl.pallas_call(
        body,
        name=name,
        out_shape=tuple(jax.ShapeDtypeStruct(shape, F32) for shape in outs),
        in_specs=[vmem] * len(args),
        out_specs=tuple(vmem for _ in outs),
        scratch_shapes=[pltpu.VMEM(shape, F32) for shape in scratch],
    )(*args)


def flip(block, axis, bit):
    count = lax.axis_size(axis)
    return lax.ppermute(block, axis, [(i, i ^ (1 << bit)) for i in range(count)])


def tiles(count):
    return (count, N, N)


def shards(leaf_maps, leaf_fluxes):
    own_map, own_flux = leaf_maps[0, 0], leaf_fluxes[0, 0]
    mate_map, mate_flux = flip(own_map, "gy", 0), flip(own_flux, "gy", 0)
    n1, n2, n3 = len(TILES1), len(TILES2), len(TILES3)
    half = FIRST // 2
    kept1, first1, rest1, y0, w0 = call(
        merge0,
        "merge0",
        [tiles(n1), tiles(half), tiles((n1 - FIRST) // 2), (N, 5 * N), (N, N)],
        [(N, N), (N, 6 * N), (5 * N, N)],
        own_map, own_flux, mate_map, mate_flux,
    )
    got = flip(first1, "gx", 0)
    swp = flip(got, "gy", 0)
    got_r = flip(rest1, "gx", 0)
    swp_r = flip(got_r, "gy", 0)
    (x1,) = call(invert_pair, "pair1", [(2 * N, 2 * N)], [tiles(2), (N, N)], kept1, got, swp)
    kept2, first2, rest2, a1, f1 = call(
        merge1,
        "merge1",
        [tiles(n2), tiles(half), tiles((n2 - FIRST) // 2), (4 * N, 2 * N), (2 * N, N)],
        [],
        x1, kept1, got, swp, got_r, swp_r,
    )
    got = flip(first2, "gy", 1)
    swp = flip(got, "gy", 0)
    got_r = flip(rest2, "gy", 1)
    swp_r = flip(got_r, "gy", 0)
    (x2,) = call(invert_pair, "pair2", [(2 * N, 2 * N)], [tiles(2), (N, N)], kept2, got, swp)
    kept3, send3, a2, f2 = call(
        merge2,
        "merge2",
        [tiles(n3), tiles(n3 // 2), (4 * N, 2 * N), (2 * N, N)],
        [],
        x2, kept2, got, swp, got_r, swp_r,
    )
    count = lax.axis_size("gx")
    inner = [pair for i in range(1, count, 4) for pair in ((i, i + 1), (i + 1, i))]
    outer = [pair for i in range(1, count, 4) for pair in ((i, i - 1), (i + 1, i + 2))]
    got = lax.ppermute(send3, "gx", inner)
    swp = flip(got, "gy", 0)
    top, down = call(solve3, "solve3", [tiles(4), tiles(2)], [tiles(n3), (N, N)], kept3, got, swp)
    got = lax.ppermute(down, "gx", outer)
    swp = flip(got, "gy", 0)
    (out,) = call(
        descend,
        "descend",
        [(4 * N, N)],
        [(4 * N, N), (4 * N, N)],
        top, got, swp, x2, a2, f2, x1, a1, f1, y0, w0,
    )
    return out[None, None]


def solution(mesh):
    spec = P("gx", "gy", None, None)
    return jax.shard_map(shards, mesh=mesh, in_specs=(spec, spec), out_specs=spec, check_vma=False)
```

```python
import jax
import jax.numpy as jnp
from jax import lax
from jax.experimental import pallas as pl
from jax.experimental.pallas import tpu as pltpu
from jax.sharding import PartitionSpec as P


N = 128
F32 = jnp.float32
HIGH = lax.Precision.HIGHEST

SENT1 = (((0, 0), (1, 0), (1, 1)), ((0, -1), (1, -1), (4, 0), (4, 1), (4, 4), (4, -1)))
KEPT1 = ((2, 0), (2, 1), (3, 0), (3, 1), (2, 2), (3, 2), (3, 3), (2, 4), (3, 4), (2, -1), (3, -1))
SENT2 = (((0, 0), (1, 0), (1, 1)),)
HALF2 = (((2, 0), (2, 1), (3, 0), (3, 1), (0, -1), (1, -1)), ((2, 2), (3, 2), (3, 3), (2, -1), (3, -1)))
SENT3 = (((0, 0),), ((1, 0), (1, 1)), ((2, 0), (2, 1), (2, 2)))
HALF3 = (((3, 0), (3, 1), (3, 2), (3, 3)), ((0, -1), (1, -1), (2, -1), (3, -1)))


def put(batches, refs):
    return {t: (ref, i) for batch, ref in zip(batches, refs) for i, t in enumerate(batch)}


def roles():
    col = lax.axis_index("gx")
    row = lax.axis_index("gy")
    return col & 1, (col >> 1) & 1, row & 1, (row >> 1) & 1


def halves(x):
    top = x.astype(jnp.bfloat16)
    return top, (x - top.astype(F32)).astype(jnp.bfloat16)


def triple(x, y, dims):
    xh, xl = halves(x)
    yh, yl = halves(y)

    def dot(p, q):
        return lax.dot_general(p, q, (dims, ((), ())), preferred_element_type=F32)

    return dot(xh, yh) + (dot(xh, yl) + dot(xl, yh))


def mm(x, y):
    return triple(x, y, ((1,), (0,)))


def mm_nt(x, y):
    return triple(x, y, ((1,), (1,)))


def mm_tn(x, y):
    return triple(x, y, ((0,), (0,)))


def over(x, rows=8):
    return jnp.broadcast_to(x, (rows, N))


def invert(x_ref, v_ref):
    lane = lax.broadcasted_iota(jnp.int32, (8, N), 1)
    sub = lax.broadcasted_iota(jnp.int32, (8, N), 0)
    rows = [x_ref[8 * i : 8 * i + 8, :] for i in range(N // 8)]
    for j in range(N // 8):
        top = rows[j]
        inside = (lane >= 8 * j) & (lane < 8 * j + 8)
        seed = jnp.where(inside, jnp.where(lane - 8 * j == sub, 1.0, 0.0), top)
        cols = {c: over(top[:, 8 * j + c : 8 * j + c + 1]) for c in range(8)}
        panel = seed
        for k in range(0, 8, 2):
            a, b = over(cols[k][k : k + 1, :]), over(cols[k + 1][k : k + 1, :])
            d = over(cols[k + 1][k + 1 : k + 2, :])
            recip = 1.0 / (a * d - b * b)

            def pivot(x, k=k, cols=cols, a=a, b=b, d=d, recip=recip):
                t0, t1 = over(x[k : k + 1, :]), over(x[k + 1 : k + 2, :])
                s0, s1 = d * t0 - b * t1, a * t1 - b * t0
                pure = x - (cols[k] * s0 + cols[k + 1] * s1) * recip
                return jnp.where(sub == k, s0 * recip, jnp.where(sub == k + 1, s1 * recip, pure))

            panel = pivot(panel)
            cols = {c: pivot(cols[c]) for c in range(k + 2, 8)}
        low = lane < 8 * j + 8
        v_ref[8 * j : 8 * j + 8, :] = jnp.where(low, seed, 0.0)
        x_ref[8 * j : 8 * j + 8, :] = jnp.where(low, panel, 0.0)
        lines = [over(panel[k : k + 1, :]) for k in range(8)]
        for i in range(j + 1, N // 8):
            b = [over(rows[i][:, 8 * j + k : 8 * j + k + 1]) * lines[k] for k in range(8)]
            total = ((b[0] + b[1]) + (b[2] + b[3])) + ((b[4] + b[5]) + (b[6] + b[7]))
            rows[i] = jnp.where(inside, 0.0, rows[i]) - total
    x_ref[...] = lax.dot_general(
        v_ref[...], x_ref[...], (((0,), (0,)), ((), ())), precision=HIGH, preferred_element_type=F32
    )


def merge0(own_map, own_flux, mate_map, mate_flux, sent0, sent1, kept, y_ref, w_ref, x_ref, v_ref, rhs, rows):
    a0, _, b0, b1 = roles()
    mine_low = b0 == 0
    f1, h = 1 - a0, a0

    def at(side):
        return pl.ds(side * N, N) if isinstance(side, int) else pl.ds(pl.multiple_of(side * N, N), N)

    def entry(leaf, r, c):
        mine, mate = own_map[at(r), at(c)], mate_map[at(r), at(c)]
        return jnp.where(mine_low, mine, mate) if leaf == 0 else jnp.where(mine_low, mate, mine)

    def flux(leaf, r):
        mine, mate = own_flux[at(r), :], mate_flux[at(r), :]
        return jnp.where(mine_low, mine, mate) if leaf == 0 else jnp.where(mine_low, mate, mine)

    face, other = (3, 2), (2, 3)
    g_up = b1 == 0
    x_ref[...] = entry(0, 3, 3) + entry(1, 2, 2)
    owner = (0, 1, 0, 1)
    side = (f1, f1, h, h)
    for p in range(4):
        rhs[:, p * N : (p + 1) * N] = entry(owner[p], face[owner[p]], side[p])
        rows[p * N : (p + 1) * N, :] = entry(owner[p], side[p], face[owner[p]])
    rhs[:, 4 * N : 5 * N] = jnp.where(g_up, entry(1, 2, 3), entry(0, 3, 2))
    rows[4 * N : 5 * N, :] = jnp.where(g_up, entry(1, 3, 2), entry(0, 2, 3))
    rhs[:, 5 * N : 6 * N] = flux(0, 3) + flux(1, 2)
    invert(x_ref, v_ref)
    out = mm(x_ref[...], rhs[...])
    y_ref[...] = out[:, : 5 * N]
    w_ref[...] = out[:, 5 * N :]
    home = put(SENT1 + (KEPT1,), (sent0, sent1, kept))
    for q, low, high in ((0, 0, 5), (1, 1, 5), (2, 2, 4), (3, 3, 4), (4, 2, 5), (-1, 0, 5)):
        cq = 5 if q < 0 else q
        drop = mm(rows[low * N : high * N, :], out[:, cq * N : (cq + 1) * N])
        for p in range(low, high):
            value = -drop[(p - low) * N : (p - low + 1) * N, :]
            if q < 0:
                if p < 4:
                    value = value + flux(owner[p], side[p])
                else:
                    value = value + jnp.where(g_up, flux(1, 3), flux(0, 2))
            elif p < 4 and q < 4:
                if owner[p] == owner[q]:
                    value = value + entry(owner[p], side[p], side[q])
            elif p < 4:
                part = entry(owner[p], side[p], other[owner[p]])
                value = value + jnp.where(g_up if owner[p] == 1 else b1 == 1, part, 0.0)
            elif q < 4:
                part = entry(owner[q], other[owner[q]], side[q])
                value = value + jnp.where(g_up if owner[q] == 1 else b1 == 1, part, 0.0)
            else:
                value = value + jnp.where(g_up, entry(1, 3, 3), entry(0, 2, 2))
            ref, i = home[(p, q)]
            ref[i] = value


def invert_pair(own, got, x_out, scratch, cross, v_ref):
    scratch[0] = own[0] + got[0]
    cross[...] = own[1] + got[1]
    scratch[1] = own[2] + got[2]

    def step(i, carry):
        invert(scratch.at[i], v_ref)

        @pl.when(i == 0)
        def _():
            t = mm(cross[...], scratch[0])
            scratch[1] = scratch[1] - mm_nt(t, cross[...])
            cross[...] = t

        return carry

    lax.fori_loop(0, 2, step, 0)
    t, x22 = cross[...], scratch[1]
    low = mm(x22, t)
    x_out[N:, N:] = x22
    x_out[N:, :N] = -low
    x_out[:N, N:] = -mm_tn(t, x22)
    x_out[:N, :N] = scratch[0] + mm_tn(t, low)


def merge1(x, own, kept, got, sent0, half0, half1, send, a_ref, f_ref):
    core = roles()[2]
    mine = put((SENT1[1], KEPT1), (own, kept))
    theirs = put((SENT1[1],), (got,))

    def load(table, t):
        ref, i = table[t]
        return ref[i]

    for q in range(2):
        cols = slice(q * N, (q + 1) * N)
        a_ref[0:N, cols] = load(mine, (4, q))
        a_ref[N : 2 * N, cols] = load(theirs, (4, q))
        a_ref[2 * N : 3 * N, cols] = load(mine, (2, q))
        a_ref[3 * N : 4 * N, cols] = load(mine, (3, q))
        f_ref[cols, :] = load(mine, (q, -1)) + load(theirs, (q, -1))
    yt = mm(a_ref[...], x[...])
    base = {
        (0, 0): (mine, (4, 4)), (1, 1): (theirs, (4, 4)), (2, 0): (mine, (2, 4)), (3, 0): (mine, (3, 4)),
        (2, 2): (mine, (2, 2)), (3, 2): (mine, (3, 2)), (3, 3): (mine, (3, 3)),
        (0, -1): (mine, (4, -1)), (1, -1): (theirs, (4, -1)), (2, -1): (mine, (2, -1)), (3, -1): (mine, (3, -1)),
    }
    spread(SENT2 + HALF2, (sent0, half0, half1), base, load, yt, a_ref, f_ref)
    half1[5] = jnp.zeros((N, N), F32)
    pick_half(core, half0, half1, send)


def spread(batches, refs, base, load, yt, a_ref, f_ref):
    home = put(batches, refs)
    for q in (0, 1, 2, 3, -1):
        low = max(q, 0)
        if q < 0:
            drop = mm(yt, f_ref[...])
        else:
            drop = mm_nt(yt[low * N :], a_ref[q * N : (q + 1) * N, :])
        for p in range(low, 4):
            value = -drop[(p - low) * N : (p - low + 1) * N, :]
            if (p, q) in base:
                value = value + load(*base[(p, q)])
            ref, i = home[(p, q)]
            ref[i] = value


def pick_half(core, half0, half1, send):
    @pl.when(core == 0)
    def _():
        send[...] = half0[...]

    @pl.when(core == 1)
    def _():
        send[...] = half1[...]


def merge2(x, half0, half1, got, swapped, sent0, sent1, sent2, half3, half4, send, a_ref, f_ref):
    core, b1 = roles()[2:]
    table = put(HALF2, (half0, half1))
    which = {t: h for h in range(2) for t in HALF2[h]}

    def mate(t):
        i = table[t][1]
        return jnp.where(core == which[t], got[i], swapped[i])

    def mine(t):
        ref, i = table[t]
        return ref[i]

    def of(half, t):
        return jnp.where(b1 == half, mine(t), mate(t))

    for q in range(2):
        cols = slice(q * N, (q + 1) * N)
        for p in range(4):
            a_ref[p * N : (p + 1) * N, cols] = of(p // 2, (2 + p % 2, q))
        f_ref[cols, :] = mine((q, -1)) + mate((q, -1))
    yt = mm(a_ref[...], x[...])
    base = {(p, q): (p // 2, (2 + p % 2, 2 + q % 2)) for p in range(4) for q in range(p + 1) if p // 2 == q // 2}
    base.update({(p, -1): (p // 2, (2 + p % 2, -1)) for p in range(4)})
    spread(SENT3 + HALF3, (sent0, sent1, sent2, half3, half4), base, of, yt, a_ref, f_ref)
    pick_half(core, half3, half4, send)


def solve_0(own, got, x_out, v_ref):
    x_out[...] = own[0] + got[0]
    invert(x_out, v_ref)


def solve_1(x0, own, got, s10, low10, x_out, v_ref):
    s = own[0] + got[0]
    low = mm(s, x0[...])
    s10[...] = s
    low10[...] = low
    x_out[...] = own[1] + got[1] - mm_nt(low, s)
    invert(x_out, v_ref)


def solve_2(x0, x1, s10, low10, own2, got2, half3, half4, got, swapped, x2, a2, f2, x1_ref, a1_ref, f1,
            kept, send, xs, v_ref, l20, l21, s21, l30, l31, l32, u, v):
    _, _, core, b1 = roles()

    def mate(h, i):
        return jnp.where(core == h, got[i], swapped[i])

    s20 = own2[0] + got2[0]
    l20[...] = mm(s20, x0[...])
    s21[...] = own2[1] + got2[1] - mm_nt(l20[...], s10[...])
    l21[...] = mm(s21[...], x1[...])
    xs[0] = own2[2] + got2[2] - mm_nt(l20[...], s20) - mm_nt(l21[...], s21[...])
    s30 = half3[0] + mate(0, 0)
    l30[...] = mm(s30, x0[...])
    s31 = half3[1] + mate(0, 1) - mm_nt(l30[...], s10[...])
    l31[...] = mm(s31, x1[...])
    l32[...] = half3[2] + mate(0, 2) - mm_nt(l30[...], s20) - mm_nt(l31[...], s21[...])
    xs[1] = half3[3] + mate(0, 3) - mm_nt(l30[...], s30) - mm_nt(l31[...], s31)

    def step(i, carry):
        invert(xs.at[i], v_ref)

        @pl.when(i == 0)
        def _():
            s32 = l32[...]
            l32[...] = mm(s32, xs[0])
            xs[1] = xs[1] - mm_nt(l32[...], s32)

        return carry

    lax.fori_loop(0, 2, step, 0)
    f = [half4[i] + mate(1, i) for i in range(4)]
    f[1] = f[1] - mm(low10[...], f[0])
    f[2] = f[2] - mm(l20[...], f[0]) - mm(l21[...], f[1])
    f[3] = f[3] - mm(l30[...], f[0]) - mm(l31[...], f[1]) - mm(l32[...], f[2])
    w3 = mm(xs[1], f[3])
    w2 = mm(xs[0], f[2]) - mm_tn(l32[...], w3)
    w1 = mm(x1[...], f[1]) - mm_tn(l31[...], w3) - mm_tn(l21[...], w2)
    w0 = mm(x0[...], f[0]) - mm_tn(l30[...], w3) - mm_tn(l20[...], w2) - mm_tn(low10[...], w1)
    for i, w in enumerate((w0, w1, w2, w3)):
        u[i * N : (i + 1) * N, :] = -w
    face2 = -mm(x2[...], mm_tn(a2[...], u[...]) + f2[...])
    v[: 2 * N, :] = face2
    v[2 * N :, :] = jnp.where(b1 == 0, u[: 2 * N, :], u[2 * N :, :])
    face1 = -mm(x1_ref[...], mm_tn(a1_ref[...], v[...]) + f1[...])
    kept[: 2 * N, :] = face1
    kept[2 * N : 4 * N, :] = v[2 * N :, :]
    kept[4 * N :, :] = face2[:N, :]
    send[: 2 * N, :] = face1
    send[2 * N :, :] = face2[N:, :]


def descend(kept, got, y0, w0, out):
    a0, a1, b0, b1 = roles()
    inner = (a0 ^ a1) == 1
    face1 = jnp.where(inner, kept[: 2 * N, :], got[: 2 * N, :])
    side_h = jnp.where(inner, kept[2 * N : 4 * N, :], 0.0)
    side_g = jnp.where(inner, kept[4 * N :, :], got[2 * N :, :])
    face0 = -(mm(y0[...], jnp.concatenate([face1, side_h, side_g], axis=0)) + w0[...])
    mine_1 = jnp.where(b0 == 0, face1[:N, :], face1[N:, :])
    mine_h = jnp.where(b0 == 0, side_h[:N, :], side_h[N:, :])
    mine_g = jnp.where((b0 ^ b1) == 1, side_g, 0.0)
    out[:N, :] = jnp.where(a0 == 0, mine_h, mine_1)
    out[N : 2 * N, :] = jnp.where(a0 == 0, mine_1, mine_h)
    out[2 * N : 3 * N, :] = jnp.where(b0 == 0, mine_g, face0)
    out[3 * N :, :] = jnp.where(b0 == 0, face0, mine_g)


def call(body, outs, scratch, tiles_of_work, *args):
    vmem = pl.BlockSpec(memory_space=pltpu.VMEM)
    return pl.pallas_call(
        body,
        out_shape=tuple(jax.ShapeDtypeStruct(shape, F32) for shape in outs),
        in_specs=[vmem] * len(args),
        out_specs=tuple(vmem for _ in outs),
        scratch_shapes=[pltpu.VMEM(shape, F32) for shape in scratch],
        cost_estimate=pl.CostEstimate(flops=tiles_of_work * 10**9, bytes_accessed=tiles_of_work * 10**6, transcendentals=0),
    )(*args)


def flip(block, axis, bit):
    count = lax.axis_size(axis)
    return lax.ppermute(block, axis, [(i, i ^ (1 << bit)) for i in range(count)])


def tiles(count):
    return (count, N, N)


def shards(leaf_maps, leaf_fluxes):
    own_map, own_flux = leaf_maps[0, 0], leaf_fluxes[0, 0]
    mate_map, mate_flux = flip(own_map, "gy", 0), flip(own_flux, "gy", 0)
    count = lax.axis_size("gx")
    inward = [pair for i in range(0, count, 4) for pair in ((i, i + 1), (i + 3, i + 2))]
    outward = [(b, a) for a, b in inward]
    inner = [pair for i in range(1, count, 4) for pair in ((i, i + 1), (i + 1, i))]
    square, wide = (N, N), (4 * N, 2 * N)

    s1a, s1b, kept1, y0, w0 = call(
        merge0,
        [tiles(3), tiles(6), tiles(len(KEPT1)), (N, 5 * N), square],
        [square, square, (N, 6 * N), (5 * N, N)],
        2,
        own_map, own_flux, mate_map, mate_flux,
    )
    g1a = lax.ppermute(s1a, "gx", inward)
    g1b = lax.ppermute(s1b, "gx", inward)
    (x1,) = call(invert_pair, [(2 * N, 2 * N)], [tiles(2), square, square], 12, s1a, g1a)
    s2a, h2a, h2b, c2, a1, f1 = call(
        merge1,
        [tiles(3), tiles(6), tiles(6), tiles(6), wide, (2 * N, N)],
        [],
        2,
        x1, s1b, kept1, g1b,
    )
    g2a = flip(s2a, "gy", 1)
    g2b = flip(c2, "gy", 1)
    (x2,) = call(invert_pair, [(2 * N, 2 * N)], [tiles(2), square, square], 12, s2a, g2a)
    g2c = flip(g2b, "gy", 0)
    s3a, s3b, s3c, h3a, h3b, c3, a2, f2 = call(
        merge2,
        [tiles(1), tiles(2), tiles(3), tiles(4), tiles(4), tiles(4), wide, (2 * N, N)],
        [],
        2,
        x2, h2a, h2b, g2b, g2c,
    )
    g3a = lax.ppermute(s3a, "gx", inner)
    g3b = lax.ppermute(s3b, "gx", inner)
    g3c = lax.ppermute(s3c, "gx", inner)
    g3d = lax.ppermute(c3, "gx", inner)
    (z0,) = call(solve_0, [square], [square], 6, s3a, g3a)
    s10, low10, z1 = call(solve_1, [square] * 3, [square], 6, z0, s3b, g3b)
    g3e = flip(g3d, "gy", 0)
    kept, send = call(
        solve_2,
        [(5 * N, N), (3 * N, N)],
        [tiles(2)] + [square] * 7 + [(4 * N, N), (4 * N, N)],
        14,
        z0, z1, s10, low10, s3c, g3c, h3a, h3b, g3d, g3e, x2, a2, f2, x1, a1, f1,
    )
    down = lax.ppermute(send, "gx", outward)
    (out,) = call(descend, [(4 * N, N)], [], 1, kept, down, y0, w0)
    return out[None, None]


def solution(mesh):
    spec = P("gx", "gy", None, None)

    return jax.shard_map(shards, mesh=mesh, in_specs=(spec, spec), out_specs=spec, check_vma=False)
```

```python
import jax
import jax.numpy as jnp
from jax import lax
from jax.experimental import pallas as pl
from jax.experimental.pallas import tpu as pltpu
from jax.sharding import PartitionSpec as P


N = 128
F32 = jnp.float32
HIGH = lax.Precision.HIGHEST

SENT1 = (((0, 0), (1, 0), (1, 1)), ((0, -1), (1, -1), (4, 0), (4, 1), (4, 4), (4, -1)))
KEPT1 = ((2, 0), (2, 1), (3, 0), (3, 1), (2, 2), (3, 2), (3, 3), (2, 4), (3, 4), (2, -1), (3, -1))
SENT2 = (((0, 0), (1, 0), (1, 1)),)
HALF2 = (((2, 0), (2, 1), (3, 0), (3, 1), (0, -1), (1, -1)), ((2, 2), (3, 2), (3, 3), (2, -1), (3, -1)))
SENT3 = (((0, 0), (1, 0), (1, 1)),)
HALF3 = (
    ((2, 0), (2, 1), (2, 2), (3, 0), (3, 1), (3, 2), (3, 3)),
    ((2, 0), (2, 1), (2, 2), (0, -1), (1, -1), (2, -1), (3, -1)),
)


def put(batches, refs):
    return {t: (ref, i) for batch, ref in zip(batches, refs) for i, t in enumerate(batch)}


def roles():
    col = lax.axis_index("gx")
    row = lax.axis_index("gy")
    return col & 1, (col >> 1) & 1, row & 1, (row >> 1) & 1


def halves(x):
    top = x.astype(jnp.bfloat16)
    return top, (x - top.astype(F32)).astype(jnp.bfloat16)


def triple(x, y, dims):
    xh, xl = halves(x)
    yh, yl = halves(y)

    def dot(p, q):
        return lax.dot_general(p, q, (dims, ((), ())), preferred_element_type=F32)

    return dot(xh, yh) + (dot(xh, yl) + dot(xl, yh))


def mm(x, y):
    return triple(x, y, ((1,), (0,)))


def mm_nt(x, y):
    return triple(x, y, ((1,), (1,)))


def mm_tn(x, y):
    return triple(x, y, ((0,), (0,)))


def over(x, rows=8):
    return jnp.broadcast_to(x, (rows, N))


def invert(x_ref, v_ref):
    lane = lax.broadcasted_iota(jnp.int32, (8, N), 1)
    sub = lax.broadcasted_iota(jnp.int32, (8, N), 0)
    rows = [x_ref[8 * i : 8 * i + 8, :] for i in range(N // 8)]
    for j in range(N // 8):
        top = rows[j]
        inside = (lane >= 8 * j) & (lane < 8 * j + 8)
        seed = jnp.where(inside, jnp.where(lane - 8 * j == sub, 1.0, 0.0), top)
        cols = {c: over(top[:, 8 * j + c : 8 * j + c + 1]) for c in range(8)}
        panel = seed
        for k in range(0, 8, 2):
            a, b = over(cols[k][k : k + 1, :]), over(cols[k + 1][k : k + 1, :])
            d = over(cols[k + 1][k + 1 : k + 2, :])
            recip = 1.0 / (a * d - b * b)

            def pivot(x, k=k, cols=cols, a=a, b=b, d=d, recip=recip):
                t0, t1 = over(x[k : k + 1, :]), over(x[k + 1 : k + 2, :])
                s0, s1 = d * t0 - b * t1, a * t1 - b * t0
                pure = x - (cols[k] * s0 + cols[k + 1] * s1) * recip
                return jnp.where(sub == k, s0 * recip, jnp.where(sub == k + 1, s1 * recip, pure))

            panel = pivot(panel)
            cols = {c: pivot(cols[c]) for c in range(k + 2, 8)}
        low = lane < 8 * j + 8
        v_ref[8 * j : 8 * j + 8, :] = jnp.where(low, seed, 0.0)
        x_ref[8 * j : 8 * j + 8, :] = jnp.where(low, panel, 0.0)
        lines = [over(panel[k : k + 1, :]) for k in range(8)]
        for i in range(j + 1, N // 8):
            b = [over(rows[i][:, 8 * j + k : 8 * j + k + 1]) * lines[k] for k in range(8)]
            total = ((b[0] + b[1]) + (b[2] + b[3])) + ((b[4] + b[5]) + (b[6] + b[7]))
            rows[i] = jnp.where(inside, 0.0, rows[i]) - total
    x_ref[...] = lax.dot_general(
        v_ref[...], x_ref[...], (((0,), (0,)), ((), ())), precision=HIGH, preferred_element_type=F32
    )


def merge0(own_map, own_flux, mate_map, mate_flux, sent0, sent1, kept, y_ref, w_ref, x_ref, v_ref, rhs, rows):
    a0, _, b0, b1 = roles()
    mine_low = b0 == 0
    f1, h = 1 - a0, a0

    def at(side):
        return pl.ds(side * N, N) if isinstance(side, int) else pl.ds(pl.multiple_of(side * N, N), N)

    def entry(leaf, r, c):
        mine, mate = own_map[at(r), at(c)], mate_map[at(r), at(c)]
        return jnp.where(mine_low, mine, mate) if leaf == 0 else jnp.where(mine_low, mate, mine)

    def flux(leaf, r):
        mine, mate = own_flux[at(r), :], mate_flux[at(r), :]
        return jnp.where(mine_low, mine, mate) if leaf == 0 else jnp.where(mine_low, mate, mine)

    face, other = (3, 2), (2, 3)
    g_up = b1 == 0
    x_ref[...] = entry(0, 3, 3) + entry(1, 2, 2)
    owner = (0, 1, 0, 1)
    side = (f1, f1, h, h)
    for p in range(4):
        rhs[:, p * N : (p + 1) * N] = entry(owner[p], face[owner[p]], side[p])
        rows[p * N : (p + 1) * N, :] = entry(owner[p], side[p], face[owner[p]])
    rhs[:, 4 * N : 5 * N] = jnp.where(g_up, entry(1, 2, 3), entry(0, 3, 2))
    rows[4 * N : 5 * N, :] = jnp.where(g_up, entry(1, 3, 2), entry(0, 2, 3))
    rhs[:, 5 * N : 6 * N] = flux(0, 3) + flux(1, 2)
    invert(x_ref, v_ref)
    out = mm(x_ref[...], rhs[...])
    y_ref[...] = out[:, : 5 * N]
    w_ref[...] = out[:, 5 * N :]
    home = put(SENT1 + (KEPT1,), (sent0, sent1, kept))
    for q, low, high in ((0, 0, 5), (1, 1, 5), (2, 2, 4), (3, 3, 4), (4, 2, 5), (-1, 0, 5)):
        cq = 5 if q < 0 else q
        drop = mm(rows[low * N : high * N, :], out[:, cq * N : (cq + 1) * N])
        for p in range(low, high):
            value = -drop[(p - low) * N : (p - low + 1) * N, :]
            if q < 0:
                if p < 4:
                    value = value + flux(owner[p], side[p])
                else:
                    value = value + jnp.where(g_up, flux(1, 3), flux(0, 2))
            elif p < 4 and q < 4:
                if owner[p] == owner[q]:
                    value = value + entry(owner[p], side[p], side[q])
            elif p < 4:
                part = entry(owner[p], side[p], other[owner[p]])
                value = value + jnp.where(g_up if owner[p] == 1 else b1 == 1, part, 0.0)
            elif q < 4:
                part = entry(owner[q], other[owner[q]], side[q])
                value = value + jnp.where(g_up if owner[q] == 1 else b1 == 1, part, 0.0)
            else:
                value = value + jnp.where(g_up, entry(1, 3, 3), entry(0, 2, 2))
            ref, i = home[(p, q)]
            ref[i] = value


def invert_pair(own, got, x_out, scratch, cross, v_ref):
    scratch[0] = own[0] + got[0]
    cross[...] = own[1] + got[1]
    scratch[1] = own[2] + got[2]

    def step(i, carry):
        invert(scratch.at[i], v_ref)

        @pl.when(i == 0)
        def _():
            t = mm(cross[...], scratch[0])
            scratch[1] = scratch[1] - mm_nt(t, cross[...])
            cross[...] = t

        return carry

    lax.fori_loop(0, 2, step, 0)
    t, x22 = cross[...], scratch[1]
    low = mm(x22, t)
    x_out[N:, N:] = x22
    x_out[N:, :N] = -low
    x_out[:N, N:] = -mm_tn(t, x22)
    x_out[:N, :N] = scratch[0] + mm_tn(t, low)


def merge1(x, own, kept, got, sent0, half0, half1, send, a_ref, f_ref):
    core = roles()[2]
    mine = put((SENT1[1], KEPT1), (own, kept))
    theirs = put((SENT1[1],), (got,))

    def load(table, t):
        ref, i = table[t]
        return ref[i]

    for q in range(2):
        cols = slice(q * N, (q + 1) * N)
        a_ref[0:N, cols] = load(mine, (4, q))
        a_ref[N : 2 * N, cols] = load(theirs, (4, q))
        a_ref[2 * N : 3 * N, cols] = load(mine, (2, q))
        a_ref[3 * N : 4 * N, cols] = load(mine, (3, q))
        f_ref[cols, :] = load(mine, (q, -1)) + load(theirs, (q, -1))
    yt = mm(a_ref[...], x[...])
    base = {
        (0, 0): (mine, (4, 4)), (1, 1): (theirs, (4, 4)), (2, 0): (mine, (2, 4)), (3, 0): (mine, (3, 4)),
        (2, 2): (mine, (2, 2)), (3, 2): (mine, (3, 2)), (3, 3): (mine, (3, 3)),
        (0, -1): (mine, (4, -1)), (1, -1): (theirs, (4, -1)), (2, -1): (mine, (2, -1)), (3, -1): (mine, (3, -1)),
    }
    spread(SENT2 + HALF2, (sent0, half0, half1), base, load, yt, a_ref, f_ref)
    half1[5] = jnp.zeros((N, N), F32)
    pick_half(core, half0, half1, send)


def spread(batches, refs, base, load, yt, a_ref, f_ref):
    for q in (0, 1, 2, 3, -1):
        low = max(q, 0)
        if q < 0:
            drop = mm(yt, f_ref[...])
        else:
            drop = mm_nt(yt[low * N :], a_ref[q * N : (q + 1) * N, :])
        for p in range(low, 4):
            value = -drop[(p - low) * N : (p - low + 1) * N, :]
            if (p, q) in base:
                value = value + load(*base[(p, q)])
            for batch, ref in zip(batches, refs):
                if (p, q) in batch:
                    ref[batch.index((p, q))] = value


def pick_half(core, half0, half1, send):
    @pl.when(core == 0)
    def _():
        send[...] = half0[...]

    @pl.when(core == 1)
    def _():
        send[...] = half1[...]


def merge2(x, half0, half1, got, swapped, sent0, half3, half4, send, a_ref, f_ref):
    core, b1 = roles()[2:]
    table = put(HALF2, (half0, half1))
    which = {t: h for h in range(2) for t in HALF2[h]}

    def mate(t):
        i = table[t][1]
        return jnp.where(core == which[t], got[i], swapped[i])

    def mine(t):
        ref, i = table[t]
        return ref[i]

    def of(half, t):
        return jnp.where(b1 == half, mine(t), mate(t))

    for q in range(2):
        cols = slice(q * N, (q + 1) * N)
        for p in range(4):
            a_ref[p * N : (p + 1) * N, cols] = of(p // 2, (2 + p % 2, q))
        f_ref[cols, :] = mine((q, -1)) + mate((q, -1))
    yt = mm(a_ref[...], x[...])
    base = {(p, q): (p // 2, (2 + p % 2, 2 + q % 2)) for p in range(4) for q in range(p + 1) if p // 2 == q // 2}
    base.update({(p, -1): (p // 2, (2 + p % 2, -1)) for p in range(4)})
    spread(SENT3 + HALF3, (sent0, half3, half4), base, of, yt, a_ref, f_ref)
    pick_half(core, half3, half4, send)


def solve_low(own, got, x0, x1, s10, low10, v_ref, xs):
    xs[0] = own[0] + got[0]
    s10[...] = own[1] + got[1]
    xs[1] = own[2] + got[2]

    def step(i, carry):
        invert(xs.at[i], v_ref)

        @pl.when(i == 0)
        def _():
            low10[...] = mm(s10[...], xs[0])
            xs[1] = xs[1] - mm_nt(low10[...], s10[...])

        return carry

    lax.fori_loop(0, 2, step, 0)
    x0[...] = xs[0]
    x1[...] = xs[1]


def solve_high(x0, x1, s10, low10, half3, half4, got, swapped, x2, a2, f2, x1_ref, a1_ref, f1,
               kept, send, xs, v_ref, l20, l21, s21, l30, l31, l32, u, v):
    _, _, core, b1 = roles()

    def mate(h, i):
        return jnp.where(core == h, got[i], swapped[i])

    s20 = half3[0] + got[0]
    l20[...] = mm(s20, x0[...])
    s21[...] = half3[1] + got[1] - mm_nt(l20[...], s10[...])
    l21[...] = mm(s21[...], x1[...])
    xs[0] = half3[2] + got[2] - mm_nt(l20[...], s20) - mm_nt(l21[...], s21[...])
    s30 = half3[3] + mate(0, 3)
    l30[...] = mm(s30, x0[...])
    s31 = half3[4] + mate(0, 4) - mm_nt(l30[...], s10[...])
    l31[...] = mm(s31, x1[...])
    l32[...] = half3[5] + mate(0, 5) - mm_nt(l30[...], s20) - mm_nt(l31[...], s21[...])
    xs[1] = half3[6] + mate(0, 6) - mm_nt(l30[...], s30) - mm_nt(l31[...], s31)

    def step(i, carry):
        invert(xs.at[i], v_ref)

        @pl.when(i == 0)
        def _():
            s32 = l32[...]
            l32[...] = mm(s32, xs[0])
            xs[1] = xs[1] - mm_nt(l32[...], s32)

        return carry

    lax.fori_loop(0, 2, step, 0)
    f = [half4[3 + i] + mate(1, 3 + i) for i in range(4)]
    f[1] = f[1] - mm(low10[...], f[0])
    f[2] = f[2] - mm(l20[...], f[0]) - mm(l21[...], f[1])
    f[3] = f[3] - mm(l30[...], f[0]) - mm(l31[...], f[1]) - mm(l32[...], f[2])
    w3 = mm(xs[1], f[3])
    w2 = mm(xs[0], f[2]) - mm_tn(l32[...], w3)
    w1 = mm(x1[...], f[1]) - mm_tn(l31[...], w3) - mm_tn(l21[...], w2)
    w0 = mm(x0[...], f[0]) - mm_tn(l30[...], w3) - mm_tn(l20[...], w2) - mm_tn(low10[...], w1)
    for i, w in enumerate((w0, w1, w2, w3)):
        u[i * N : (i + 1) * N, :] = -w
    face2 = -mm(x2[...], mm_tn(a2[...], u[...]) + f2[...])
    v[: 2 * N, :] = face2
    v[2 * N :, :] = jnp.where(b1 == 0, u[: 2 * N, :], u[2 * N :, :])
    face1 = -mm(x1_ref[...], mm_tn(a1_ref[...], v[...]) + f1[...])
    kept[: 2 * N, :] = face1
    kept[2 * N : 4 * N, :] = v[2 * N :, :]
    kept[4 * N :, :] = face2[:N, :]
    send[: 2 * N, :] = face1
    send[2 * N :, :] = face2[N:, :]


def descend(kept, got, y0, w0, out):
    a0, a1, b0, b1 = roles()
    inner = (a0 ^ a1) == 1
    face1 = jnp.where(inner, kept[: 2 * N, :], got[: 2 * N, :])
    side_h = jnp.where(inner, kept[2 * N : 4 * N, :], 0.0)
    side_g = jnp.where(inner, kept[4 * N :, :], got[2 * N :, :])
    face0 = -(mm(y0[...], jnp.concatenate([face1, side_h, side_g], axis=0)) + w0[...])
    mine_1 = jnp.where(b0 == 0, face1[:N, :], face1[N:, :])
    mine_h = jnp.where(b0 == 0, side_h[:N, :], side_h[N:, :])
    mine_g = jnp.where((b0 ^ b1) == 1, side_g, 0.0)
    out[:N, :] = jnp.where(a0 == 0, mine_h, mine_1)
    out[N : 2 * N, :] = jnp.where(a0 == 0, mine_1, mine_h)
    out[2 * N : 3 * N, :] = jnp.where(b0 == 0, mine_g, face0)
    out[3 * N :, :] = jnp.where(b0 == 0, face0, mine_g)


def call(body, outs, scratch, tiles_of_work, *args):
    vmem = pl.BlockSpec(memory_space=pltpu.VMEM)
    return pl.pallas_call(
        body,
        out_shape=tuple(jax.ShapeDtypeStruct(shape, F32) for shape in outs),
        in_specs=[vmem] * len(args),
        out_specs=tuple(vmem for _ in outs),
        scratch_shapes=[pltpu.VMEM(shape, F32) for shape in scratch],
        compiler_params=pltpu.CompilerParams(vmem_limit_bytes=12 * 2**20),
        cost_estimate=pl.CostEstimate(flops=tiles_of_work * 10**9, bytes_accessed=tiles_of_work * 10**6, transcendentals=0),
    )(*args)


def flip(block, axis, bit):
    count = lax.axis_size(axis)
    return lax.ppermute(block, axis, [(i, i ^ (1 << bit)) for i in range(count)])


def tiles(count):
    return (count, N, N)


def shards(leaf_maps, leaf_fluxes):
    own_map, own_flux = leaf_maps[0, 0], leaf_fluxes[0, 0]
    mate_map, mate_flux = flip(own_map, "gy", 0), flip(own_flux, "gy", 0)
    count = lax.axis_size("gx")
    inward = [pair for i in range(0, count, 4) for pair in ((i, i + 1), (i + 3, i + 2))]
    outward = [(b, a) for a, b in inward]
    inner = [pair for i in range(1, count, 4) for pair in ((i, i + 1), (i + 1, i))]
    square, wide = (N, N), (4 * N, 2 * N)

    s1a, s1b, kept1, y0, w0 = call(
        merge0,
        [tiles(3), tiles(6), tiles(len(KEPT1)), (N, 5 * N), square],
        [square, square, (N, 6 * N), (5 * N, N)],
        2,
        own_map, own_flux, mate_map, mate_flux,
    )
    g1a = lax.ppermute(s1a, "gx", inward)
    g1b = lax.ppermute(s1b, "gx", inward)
    (x1,) = call(invert_pair, [(2 * N, 2 * N)], [tiles(2), square, square], 12, s1a, g1a)
    s2a, h2a, h2b, c2, a1, f1 = call(
        merge1,
        [tiles(3), tiles(6), tiles(6), tiles(6), wide, (2 * N, N)],
        [],
        2,
        x1, s1b, kept1, g1b,
    )
    g2a = flip(s2a, "gy", 1)
    g2b = flip(c2, "gy", 1)
    (x2,) = call(invert_pair, [(2 * N, 2 * N)], [tiles(2), square, square], 12, s2a, g2a)
    g2c = flip(g2b, "gy", 0)
    s3a, h3a, h3b, c3, a2, f2 = call(
        merge2,
        [tiles(3), tiles(7), tiles(7), tiles(7), wide, (2 * N, N)],
        [],
        2,
        x2, h2a, h2b, g2b, g2c,
    )
    g3a = lax.ppermute(s3a, "gx", inner)
    g3b = lax.ppermute(c3, "gx", inner)
    z0, z1, s10, low10 = call(solve_low, [square] * 4, [square, tiles(2)], 12, s3a, g3a)
    g3c = flip(g3b, "gy", 0)
    kept, send = call(
        solve_high,
        [(5 * N, N), (3 * N, N)],
        [tiles(2)] + [square] * 7 + [(4 * N, N), (4 * N, N)],
        14,
        z0, z1, s10, low10, h3a, h3b, g3b, g3c, x2, a2, f2, x1, a1, f1,
    )
    down = lax.ppermute(send, "gx", outward)
    (out,) = call(descend, [(4 * N, N)], [], 1, kept, down, y0, w0)
    return out[None, None]


def solution(mesh):
    spec = P("gx", "gy", None, None)

    return jax.shard_map(shards, mesh=mesh, in_specs=(spec, spec), out_specs=spec, check_vma=False)
```

```python
import jax
import jax.numpy as jnp
from jax import lax
from jax.experimental import pallas as pl
from jax.experimental.pallas import tpu as pltpu
from jax.sharding import PartitionSpec as P


N = 128
F32 = jnp.float32

FACE = (((0, 0),), ((1, 0), (1, 1)))
SENT1 = ((0, -1), (1, -1), (4, 0), (4, 1), (4, 4), (4, -1))
KEPT1 = ((2, 0), (2, 1), (3, 0), (3, 1), (2, 2), (3, 2), (3, 3), (2, 4), (3, 4), (2, -1), (3, -1))
HALF2 = (((2, 0), (2, 1), (3, 0), (3, 1), (0, -1), (1, -1)), ((2, 2), (3, 2), (3, 3), (2, -1), (3, -1)))
SENT3 = (((0, 0),), ((1, 0), (1, 1), (2, 0), (2, 1), (2, 2)))
HALF3 = (((3, 0), (3, 1), (3, 2), (3, 3)), ((0, -1), (1, -1), (2, -1), (3, -1)))


def put(batches, refs):
    return {t: (ref, i) for batch, ref in zip(batches, refs) for i, t in enumerate(batch)}


def roles():
    col = lax.axis_index("gx")
    row = lax.axis_index("gy")
    return col & 1, (col >> 1) & 1, row & 1, (row >> 1) & 1


def halves(x):
    top = x.astype(jnp.bfloat16)
    return top, (x - top.astype(F32)).astype(jnp.bfloat16)


def triple(x, y, dims):
    xh, xl = halves(x)
    yh, yl = halves(y)

    def dot(p, q):
        return lax.dot_general(p, q, (dims, ((), ())), preferred_element_type=F32)

    return dot(xh, yh) + (dot(xh, yl) + dot(xl, yh))


def mm(x, y):
    return triple(x, y, ((1,), (0,)))


def mm_nt(x, y):
    return triple(x, y, ((1,), (1,)))


def mm_tn(x, y):
    return triple(x, y, ((0,), (0,)))


def over(x, rows=8):
    return jnp.broadcast_to(x, (rows, N))


def invert(x_ref, v_ref):
    lane = lax.broadcasted_iota(jnp.int32, (8, N), 1)
    sub = lax.broadcasted_iota(jnp.int32, (8, N), 0)
    rows = [x_ref[8 * i : 8 * i + 8, :] for i in range(N // 8)]
    for j in range(N // 8):
        top = rows[j]
        inside = (lane >= 8 * j) & (lane < 8 * j + 8)
        seed = jnp.where(inside, jnp.where(lane - 8 * j == sub, 1.0, 0.0), top)
        cols = {c: over(top[:, 8 * j + c : 8 * j + c + 1]) for c in range(8)}
        panel = seed
        for k in range(0, 8, 2):
            a, b = over(cols[k][k : k + 1, :]), over(cols[k + 1][k : k + 1, :])
            d = over(cols[k + 1][k + 1 : k + 2, :])
            recip = 1.0 / (a * d - b * b)

            def pivot(x, k=k, cols=cols, a=a, b=b, d=d, recip=recip):
                t0, t1 = over(x[k : k + 1, :]), over(x[k + 1 : k + 2, :])
                s0, s1 = d * t0 - b * t1, a * t1 - b * t0
                pure = x - (cols[k] * s0 + cols[k + 1] * s1) * recip
                return jnp.where(sub == k, s0 * recip, jnp.where(sub == k + 1, s1 * recip, pure))

            panel = pivot(panel)
            cols = {c: pivot(cols[c]) for c in range(k + 2, 8)}
        low = lane < 8 * j + 8
        v_ref[8 * j : 8 * j + 8, :] = jnp.where(low, seed, 0.0)
        x_ref[8 * j : 8 * j + 8, :] = jnp.where(low, panel, 0.0)
        lines = [over(panel[k : k + 1, :]) for k in range(8)]
        for i in range(j + 1, N // 8):
            b = [over(rows[i][:, 8 * j + k : 8 * j + k + 1]) * lines[k] for k in range(8)]
            total = ((b[0] + b[1]) + (b[2] + b[3])) + ((b[4] + b[5]) + (b[6] + b[7]))
            rows[i] = jnp.where(inside, 0.0, rows[i]) - total
    x_ref[...] = mm_tn(v_ref[...], x_ref[...])


class Leaves:
    def __init__(self, own_map, mate_map, own_flux=None, mate_flux=None):
        a0, _, b0, b1 = roles()
        self.maps, self.fluxes = (own_map, mate_map), (own_flux, mate_flux)
        self.mine_low, self.g_up = b0 == 0, b1 == 0
        self.f1, self.h = 1 - a0, a0

    def pick(self, leaf, mine, mate):
        return jnp.where(self.mine_low, mine, mate) if leaf == 0 else jnp.where(self.mine_low, mate, mine)

    def entry(self, leaf, r, c):
        return self.pick(leaf, *(ref[at(r), at(c)] for ref in self.maps))

    def flux(self, leaf, r):
        return self.pick(leaf, *(ref[at(r), :] for ref in self.fluxes))


def at(side):
    return pl.ds(side * N, N) if isinstance(side, int) else pl.ds(pl.multiple_of(side * N, N), N)


def fetch(own_map, own_flux, map_out, flux_out):
    map_out[...] = own_map[...]
    flux_out[...] = own_flux[...]


def merge0(map_out, mate_map, x_ref, face0, face1, v_ref):
    a0, _, b0, _ = roles()
    low = b0 == 0
    f1, mine, his = 1 - a0, 3 - b0, 2 + b0
    x_ref[...] = map_out[at(mine), at(mine)] + mate_map[at(his), at(his)]
    invert(x_ref, v_ref)
    ours = (map_out[at(mine), at(f1)], map_out[at(f1), at(mine)], map_out[at(f1), at(f1)])
    theirs = (mate_map[at(his), at(f1)], mate_map[at(f1), at(his)], mate_map[at(f1), at(f1)])
    lower = [jnp.where(low, o, t) for o, t in zip(ours, theirs)]
    upper = [jnp.where(low, t, o) for o, t in zip(ours, theirs)]
    y_low, y_up = mm(x_ref[...], lower[0]), mm(x_ref[...], upper[0])
    face0[0] = lower[2] - mm(lower[1], y_low)
    face1[0] = -mm(upper[1], y_low)
    face1[1] = upper[2] - mm(upper[1], y_up)


def merge0_rest(own_map, own_flux, mate_map, mate_flux, x_ref, sent, kept, y_ref, w_ref, rhs, rows):
    leaves = Leaves(own_map, mate_map, own_flux, mate_flux)
    entry, flux, g_up = leaves.entry, leaves.flux, leaves.g_up
    face, other = (3, 2), (2, 3)
    owner = (0, 1, 0, 1)
    side = (leaves.f1, leaves.f1, leaves.h, leaves.h)
    for p in range(4):
        rhs[:, p * N : (p + 1) * N] = entry(owner[p], face[owner[p]], side[p])
        rows[p * N : (p + 1) * N, :] = entry(owner[p], side[p], face[owner[p]])
    rhs[:, 4 * N : 5 * N] = jnp.where(g_up, entry(1, 2, 3), entry(0, 3, 2))
    rows[4 * N : 5 * N, :] = jnp.where(g_up, entry(1, 3, 2), entry(0, 2, 3))
    rhs[:, 5 * N : 6 * N] = flux(0, 3) + flux(1, 2)
    out = mm(x_ref[...], rhs[...])
    y_ref[...] = out[:, : 5 * N]
    w_ref[...] = out[:, 5 * N :]
    home = put((SENT1, KEPT1), (sent, kept))
    for q, low, high in ((0, 2, 5), (1, 2, 5), (2, 2, 4), (3, 3, 4), (4, 2, 5), (-1, 0, 5)):
        cq = 5 if q < 0 else q
        drop = mm(rows[low * N : high * N, :], out[:, cq * N : (cq + 1) * N])
        for p in range(low, high):
            value = -drop[(p - low) * N : (p - low + 1) * N, :]
            if q < 0:
                if p < 4:
                    value = value + flux(owner[p], side[p])
                else:
                    value = value + jnp.where(g_up, flux(1, 3), flux(0, 2))
            elif p < 4 and q < 4:
                if owner[p] == owner[q]:
                    value = value + entry(owner[p], side[p], side[q])
            elif p < 4:
                part = entry(owner[p], side[p], other[owner[p]])
                value = value + jnp.where(g_up if owner[p] == 1 else jnp.logical_not(g_up), part, 0.0)
            elif q < 4:
                part = entry(owner[q], other[owner[q]], side[q])
                value = value + jnp.where(g_up if owner[q] == 1 else jnp.logical_not(g_up), part, 0.0)
            else:
                value = value + jnp.where(g_up, entry(1, 3, 3), entry(0, 2, 2))
            ref, i = home[(p, q)]
            ref[i] = value


def pair_0(own, got, x_out, v_ref):
    x_out[...] = own[0] + got[0]
    invert(x_out, v_ref)


def pair_1(x11, own, got, x_out, x22, v_ref):
    s = own[0] + got[0]
    t = mm(s, x11[...])
    x22[...] = own[1] + got[1] - mm_nt(t, s)
    invert(x22, v_ref)
    low = mm(x22[...], t)
    x_out[N:, N:] = x22[...]
    x_out[N:, :N] = -low
    x_out[:N, N:] = -mm_tn(t, x22[...])
    x_out[:N, :N] = x11[...] + mm_tn(t, low)


def load(table, t):
    ref, i = table[t]
    return ref[i]


def merge1(x, own, kept, got, face0, face1, half0, half1, send, a_ref, f_ref):
    core = roles()[2]
    mine = put((SENT1, KEPT1), (own, kept))
    theirs = put((SENT1,), (got,))
    for q in range(2):
        cols = slice(q * N, (q + 1) * N)
        a_ref[0:N, cols] = load(mine, (4, q))
        a_ref[N : 2 * N, cols] = load(theirs, (4, q))
        a_ref[2 * N : 3 * N, cols] = load(mine, (2, q))
        a_ref[3 * N : 4 * N, cols] = load(mine, (3, q))
        f_ref[cols, :] = load(mine, (q, -1)) + load(theirs, (q, -1))
    yt = mm(a_ref[...], x[...])
    base = {
        (0, 0): (mine, (4, 4)), (1, 1): (theirs, (4, 4)), (2, 0): (mine, (2, 4)), (3, 0): (mine, (3, 4)),
        (2, 2): (mine, (2, 2)), (3, 2): (mine, (3, 2)), (3, 3): (mine, (3, 3)),
        (0, -1): (mine, (4, -1)), (1, -1): (theirs, (4, -1)), (2, -1): (mine, (2, -1)), (3, -1): (mine, (3, -1)),
    }
    spread(FACE + HALF2, (face0, face1, half0, half1), base, load, yt, a_ref, f_ref)
    half1[5] = jnp.zeros((N, N), F32)
    pick_half(core, half0, half1, send)


def spread(batches, refs, base, take, yt, a_ref, f_ref):
    home = put(batches, refs)
    for q in (0, 1, 2, 3, -1):
        low = max(q, 0)
        if q < 0:
            drop = mm(yt, f_ref[...])
        else:
            drop = mm_nt(yt[low * N :], a_ref[q * N : (q + 1) * N, :])
        for p in range(low, 4):
            value = -drop[(p - low) * N : (p - low + 1) * N, :]
            if (p, q) in base:
                value = value + take(*base[(p, q)])
            ref, i = home[(p, q)]
            ref[i] = value


def pick_half(core, half0, half1, send):
    @pl.when(core == 0)
    def _():
        send[...] = half0[...]

    @pl.when(core == 1)
    def _():
        send[...] = half1[...]


def sides2(half0, half1, got, swapped):
    core, b1 = roles()[2:]
    table = put(HALF2, (half0, half1))
    which = {t: h for h in range(2) for t in HALF2[h]}

    def mate(t):
        i = table[t][1]
        return jnp.where(core == which[t], got[i], swapped[i])

    def of(half, t):
        return jnp.where(b1 == half, load(table, t), mate(t))

    def both(t):
        return load(table, t) + mate(t)

    return of, both


def merge2(x, half0, half1, got, swapped, sent0, sent1, half3, half4, send, a_ref, f_ref):
    of, both = sides2(half0, half1, got, swapped)
    for q in range(2):
        cols = slice(q * N, (q + 1) * N)
        for p in range(4):
            a_ref[p * N : (p + 1) * N, cols] = of(p // 2, (2 + p % 2, q))
        f_ref[cols, :] = both((q, -1))
    yt = mm(a_ref[...], x[...])
    base = {(p, q): (p // 2, (2 + p % 2, 2 + q % 2)) for p in range(4) for q in range(p + 1) if p // 2 == q // 2}
    base.update({(p, -1): (p // 2, (2 + p % 2, -1)) for p in range(4)})
    spread(SENT3 + HALF3, (sent0, sent1, half3, half4), base, of, yt, a_ref, f_ref)
    pick_half(roles()[2], half3, half4, send)


def solve_1(x0, own, got, s10, low10, x_out, v_ref):
    s = own[0] + got[0]
    low = mm(s, x0[...])
    s10[...] = s
    low10[...] = low
    x_out[...] = own[1] + got[1] - mm_nt(low, s)
    invert(x_out, v_ref)


def solve_2(x0, x1, s10, own, got, s20, l20, s21, l21, x_out, v_ref):
    s = own[2] + got[2]
    low = mm(s, x0[...])
    s20[...], l20[...] = s, low
    t = own[3] + got[3] - mm_nt(low, s10[...])
    u = mm(t, x1[...])
    s21[...], l21[...] = t, u
    x_out[...] = own[4] + got[4] - mm_nt(low, s) - mm_nt(u, t)
    invert(x_out, v_ref)


def solve_3(x0, x1, x2, s10, low10, s20, l20, s21, l21, half3, half4, got, swapped, xx2, a2, f2, xx1, a1, f1,
            kept, send, x3, v_ref, u, v):
    _, _, core, b1 = roles()

    def mate(h, i):
        return jnp.where(core == h, got[i], swapped[i])

    s30 = half3[0] + mate(0, 0)
    l30 = mm(s30, x0[...])
    s31 = half3[1] + mate(0, 1) - mm_nt(l30, s10[...])
    l31 = mm(s31, x1[...])
    s32 = half3[2] + mate(0, 2) - mm_nt(l30, s20[...]) - mm_nt(l31, s21[...])
    l32 = mm(s32, x2[...])
    x3[...] = half3[3] + mate(0, 3) - mm_nt(l30, s30) - mm_nt(l31, s31) - mm_nt(l32, s32)
    invert(x3, v_ref)
    f = [half4[i] + mate(1, i) for i in range(4)]
    f[1] = f[1] - mm(low10[...], f[0])
    f[2] = f[2] - mm(l20[...], f[0]) - mm(l21[...], f[1])
    f[3] = f[3] - mm(l30, f[0]) - mm(l31, f[1]) - mm(l32, f[2])
    p2, p1, p0 = mm(x2[...], f[2]), mm(x1[...], f[1]), mm(x0[...], f[0])
    w3 = mm(x3[...], f[3])
    w2 = p2 - mm_tn(l32, w3)
    w1 = p1 - mm_tn(l31, w3) - mm_tn(l21[...], w2)
    w0 = p0 - mm_tn(l30, w3) - mm_tn(l20[...], w2) - mm_tn(low10[...], w1)
    for i, w in enumerate((w0, w1, w2, w3)):
        u[i * N : (i + 1) * N, :] = -w
    face2 = -mm(xx2[...], mm_tn(a2[...], u[...]) + f2[...])
    v[: 2 * N, :] = face2
    v[2 * N :, :] = jnp.where(b1 == 0, u[: 2 * N, :], u[2 * N :, :])
    face1 = -mm(xx1[...], mm_tn(a1[...], v[...]) + f1[...])
    kept[: 2 * N, :] = face1
    kept[2 * N : 4 * N, :] = v[2 * N :, :]
    kept[4 * N :, :] = face2[:N, :]
    send[: 2 * N, :] = face1
    send[2 * N :, :] = face2[N:, :]


def descend(kept, got, y0, w0, out):
    a0, a1, b0, b1 = roles()
    inner = (a0 ^ a1) == 1
    face1 = jnp.where(inner, kept[: 2 * N, :], got[: 2 * N, :])
    side_h = jnp.where(inner, kept[2 * N : 4 * N, :], 0.0)
    side_g = jnp.where(inner, kept[4 * N :, :], got[2 * N :, :])
    face0 = -(mm(y0[...], jnp.concatenate([face1, side_h, side_g], axis=0)) + w0[...])
    mine_1 = jnp.where(b0 == 0, face1[:N, :], face1[N:, :])
    mine_h = jnp.where(b0 == 0, side_h[:N, :], side_h[N:, :])
    mine_g = jnp.where((b0 ^ b1) == 1, side_g, 0.0)
    out[:N, :] = jnp.where(a0 == 0, mine_h, mine_1)
    out[N : 2 * N, :] = jnp.where(a0 == 0, mine_1, mine_h)
    out[2 * N : 3 * N, :] = jnp.where(b0 == 0, mine_g, face0)
    out[3 * N :, :] = jnp.where(b0 == 0, face0, mine_g)


def call(body, outs, scratch, weight, *args):
    vmem = pl.BlockSpec(memory_space=pltpu.VMEM)
    return pl.pallas_call(
        body,
        out_shape=tuple(jax.ShapeDtypeStruct(shape, F32) for shape in outs),
        in_specs=[vmem] * len(args),
        out_specs=tuple(vmem for _ in outs),
        scratch_shapes=[pltpu.VMEM(shape, F32) for shape in scratch],
        compiler_params=pltpu.CompilerParams(vmem_limit_bytes=12 * 2**20),
        cost_estimate=pl.CostEstimate(flops=weight * 10**9, bytes_accessed=weight * 10**6, transcendentals=0),
    )(*args)


def flip(block, axis, bit):
    count = lax.axis_size(axis)
    return lax.ppermute(block, axis, [(i, i ^ (1 << bit)) for i in range(count)])


def tiles(count):
    return (count, N, N)


def shards(leaf_maps, leaf_fluxes):
    own_map, own_flux = leaf_maps[0, 0], leaf_fluxes[0, 0]
    mate_map = flip(own_map, "gy", 0)
    mate_flux = flip(own_flux, "gy", 0)
    map_v, flux_v = call(fetch, [(4 * N, 4 * N), (4 * N, N)], [], 1, own_map, own_flux)
    count = lax.axis_size("gx")
    inward = [pair for i in range(0, count, 4) for pair in ((i, i + 1), (i + 3, i + 2))]
    outward = [(b, a) for a, b in inward]
    inner = [pair for i in range(1, count, 4) for pair in ((i, i + 1), (i + 1, i))]
    square, wide = (N, N), (4 * N, 2 * N)

    x0, face, face_b = call(merge0, [square, tiles(1), tiles(2)], [square], 6, map_v, mate_map)
    got_a = lax.ppermute(face, "gx", inward)
    got_b = lax.ppermute(face_b, "gx", inward)
    sent1, kept1, y0, w0 = call(
        merge0_rest, [tiles(6), tiles(len(KEPT1)), (N, 5 * N), square], [(N, 6 * N), (5 * N, N)], 2,
        map_v, flux_v, mate_map, mate_flux, x0,
    )
    got_c = lax.ppermute(sent1, "gx", inward)
    (xa,) = call(pair_0, [square], [square], 6, face, got_a)
    (x1,) = call(pair_1, [(2 * N, 2 * N)], [square, square], 6, xa, face_b, got_b)

    face, face_b, h2a, h2b, sent2, a1, f1 = call(
        merge1, [tiles(1), tiles(2), tiles(6), tiles(6), tiles(6), wide, (2 * N, N)], [], 2,
        x1, sent1, kept1, got_c,
    )
    got_a = flip(face, "gy", 1)
    got_b = flip(face_b, "gy", 1)
    got_c = flip(sent2, "gy", 1)
    (xa,) = call(pair_0, [square], [square], 6, face, got_a)
    (x2,) = call(pair_1, [(2 * N, 2 * N)], [square, square], 6, xa, face_b, got_b)
    got_d = flip(got_c, "gy", 0)

    face, s3b, h3a, h3b, sent3, a2, f2 = call(
        merge2, [tiles(1), tiles(5), tiles(4), tiles(4), tiles(4), wide, (2 * N, N)], [], 2,
        x2, h2a, h2b, got_c, got_d,
    )
    got_a = lax.ppermute(face, "gx", inner)
    got_b = lax.ppermute(s3b, "gx", inner)
    (z0,) = call(pair_0, [square], [square], 6, face, got_a)
    got_c = lax.ppermute(sent3, "gx", inner)
    s10, low10, z1 = call(solve_1, [square] * 3, [square], 6, z0, s3b, got_b)
    s20, l20, s21, l21, z2 = call(solve_2, [square] * 5, [square], 7, z0, z1, s10, s3b, got_b)
    got_d = flip(got_c, "gy", 0)
    kept, send = call(
        solve_3, [(5 * N, N), (3 * N, N)], [square, square, (4 * N, N), (4 * N, N)], 10,
        z0, z1, z2, s10, low10, s20, l20, s21, l21, h3a, h3b, got_c, got_d, x2, a2, f2, x1, a1, f1,
    )
    down = lax.ppermute(send, "gx", outward)
    (out,) = call(descend, [(4 * N, N)], [], 1, kept, down, y0, w0)
    return out[None, None]


def solution(mesh):
    spec = P("gx", "gy", None, None)

    return jax.shard_map(shards, mesh=mesh, in_specs=(spec, spec), out_specs=spec, check_vma=False)
```

```python
import jax
import jax.numpy as jnp
from jax import lax
from jax.experimental import pallas as pl
from jax.experimental.pallas import tpu as pltpu
from jax.sharding import PartitionSpec as P


N = 128
F32 = jnp.float32

SENT1 = ((4, 0), (4, 1), (4, 4))
FLUX1 = ((0, -1), (1, -1), (4, -1))
KEPT1 = ((2, 0), (2, 1), (3, 0), (3, 1), (2, 2), (3, 2), (3, 3), (2, 4), (3, 4), (2, -1), (3, -1))
HALF2 = (((2, 0), (2, 1), (3, 0), (3, 1), (0, -1), (1, -1)), ((2, 2), (3, 2), (3, 3), (2, -1), (3, -1)))
SENT3 = (((0, 0),), ((1, 0), (1, 1), (2, 0), (2, 1), (2, 2)))
HALF3 = (((3, 0), (3, 1), (3, 2), (3, 3)), ((0, -1), (1, -1), (2, -1), (3, -1)))


def put(batches, refs):
    return {t: (ref, i) for batch, ref in zip(batches, refs) for i, t in enumerate(batch)}


def roles():
    col = lax.axis_index("gx")
    row = lax.axis_index("gy")
    return col & 1, (col >> 1) & 1, row & 1, (row >> 1) & 1


def halves(x):
    top = x.astype(jnp.bfloat16)
    return top, (x - top.astype(F32)).astype(jnp.bfloat16)


def triple(x, y, dims):
    xh, xl = halves(x)
    yh, yl = halves(y)

    def dot(p, q):
        return lax.dot_general(p, q, (dims, ((), ())), preferred_element_type=F32)

    return dot(xh, yh) + (dot(xh, yl) + dot(xl, yh))


def mm(x, y):
    return triple(x, y, ((1,), (0,)))


def mm_nt(x, y):
    return triple(x, y, ((1,), (1,)))


def mm_tn(x, y):
    return triple(x, y, ((0,), (0,)))


def over(x, rows=8):
    return jnp.broadcast_to(x, (rows, N))


def invert(x_ref, v_ref):
    lane = lax.broadcasted_iota(jnp.int32, (8, N), 1)
    sub = lax.broadcasted_iota(jnp.int32, (8, N), 0)
    rows = [x_ref[8 * i : 8 * i + 8, :] for i in range(N // 8)]
    for j in range(N // 8):
        top = rows[j]
        inside = (lane >= 8 * j) & (lane < 8 * j + 8)
        seed = jnp.where(inside, jnp.where(lane - 8 * j == sub, 1.0, 0.0), top)
        cols = {c: over(top[:, 8 * j + c : 8 * j + c + 1]) for c in range(8)}
        panel = seed
        for k in range(0, 8, 2):
            a, b = over(cols[k][k : k + 1, :]), over(cols[k + 1][k : k + 1, :])
            d = over(cols[k + 1][k + 1 : k + 2, :])
            recip = 1.0 / (a * d - b * b)

            def pivot(x, k=k, cols=cols, a=a, b=b, d=d, recip=recip):
                t0, t1 = over(x[k : k + 1, :]), over(x[k + 1 : k + 2, :])
                s0, s1 = d * t0 - b * t1, a * t1 - b * t0
                pure = x - (cols[k] * s0 + cols[k + 1] * s1) * recip
                return jnp.where(sub == k, s0 * recip, jnp.where(sub == k + 1, s1 * recip, pure))

            panel = pivot(panel)
            cols = {c: pivot(cols[c]) for c in range(k + 2, 8)}
        low = lane < 8 * j + 8
        v_ref[8 * j : 8 * j + 8, :] = jnp.where(low, seed, 0.0)
        x_ref[8 * j : 8 * j + 8, :] = jnp.where(low, panel, 0.0)
        lines = [over(panel[k : k + 1, :]) for k in range(8)]
        for i in range(j + 1, N // 8):
            b = [over(rows[i][:, 8 * j + k : 8 * j + k + 1]) * lines[k] for k in range(8)]
            total = ((b[0] + b[1]) + (b[2] + b[3])) + ((b[4] + b[5]) + (b[6] + b[7]))
            rows[i] = jnp.where(inside, 0.0, rows[i]) - total
    x_ref[...] = mm_tn(v_ref[...], x_ref[...])


class Leaves:
    def __init__(self, own_map, mate_map, own_flux=None, mate_flux=None):
        a0, _, b0, b1 = roles()
        self.maps, self.fluxes = (own_map, mate_map), (own_flux, mate_flux)
        self.mine_low, self.g_up = b0 == 0, b1 == 0
        self.f1, self.h = 1 - a0, a0

    def pick(self, leaf, mine, mate):
        return jnp.where(self.mine_low, mine, mate) if leaf == 0 else jnp.where(self.mine_low, mate, mine)

    def entry(self, leaf, r, c):
        return self.pick(leaf, *(ref[at(r), at(c)] for ref in self.maps))

    def flux(self, leaf, r):
        return self.pick(leaf, *(ref[at(r), :] for ref in self.fluxes))


def at(side):
    return pl.ds(side * N, N) if isinstance(side, int) else pl.ds(pl.multiple_of(side * N, N), N)


def fetch(own_map, own_flux, map_out, flux_out):
    map_out[...] = own_map[...]
    flux_out[...] = own_flux[...]


def merge0(map_out, mate_map, x_ref, face0, face1, v_ref):
    a0, _, b0, _ = roles()
    low = b0 == 0
    f1, mine, his = 1 - a0, 3 - b0, 2 + b0
    x_ref[...] = map_out[at(mine), at(mine)] + mate_map[at(his), at(his)]
    invert(x_ref, v_ref)
    ours = (map_out[at(mine), at(f1)], map_out[at(f1), at(mine)], map_out[at(f1), at(f1)])
    theirs = (mate_map[at(his), at(f1)], mate_map[at(f1), at(his)], mate_map[at(f1), at(f1)])
    lower = [jnp.where(low, o, t) for o, t in zip(ours, theirs)]
    upper = [jnp.where(low, t, o) for o, t in zip(ours, theirs)]
    y_low, y_up = mm(x_ref[...], lower[0]), mm(x_ref[...], upper[0])
    face0[0] = lower[2] - mm(lower[1], y_low)
    face1[0] = -mm(upper[1], y_low)
    face1[1] = upper[2] - mm(upper[1], y_up)


def merge0_rest(own_map, own_flux, mate_map, mate_flux, x_ref, sent, flux_sent, kept, y_ref, w_ref, rhs, rows):
    leaves = Leaves(own_map, mate_map, own_flux, mate_flux)
    entry, flux, g_up = leaves.entry, leaves.flux, leaves.g_up
    face, other = (3, 2), (2, 3)
    owner = (0, 1, 0, 1)
    side = (leaves.f1, leaves.f1, leaves.h, leaves.h)
    for p in range(4):
        rhs[:, p * N : (p + 1) * N] = entry(owner[p], face[owner[p]], side[p])
        rows[p * N : (p + 1) * N, :] = entry(owner[p], side[p], face[owner[p]])
    rhs[:, 4 * N : 5 * N] = jnp.where(g_up, entry(1, 2, 3), entry(0, 3, 2))
    rows[4 * N : 5 * N, :] = jnp.where(g_up, entry(1, 3, 2), entry(0, 2, 3))
    rhs[:, 5 * N : 6 * N] = flux(0, 3) + flux(1, 2)
    out = mm(x_ref[...], rhs[...])
    y_ref[...] = out[:, : 5 * N]
    w_ref[...] = out[:, 5 * N :]
    home = put((SENT1, FLUX1, KEPT1), (sent, flux_sent, kept))
    for q, low, high in ((0, 2, 5), (1, 2, 5), (2, 2, 4), (3, 3, 4), (4, 2, 5), (-1, 0, 5)):
        cq = 5 if q < 0 else q
        drop = mm(rows[low * N : high * N, :], out[:, cq * N : (cq + 1) * N])
        for p in range(low, high):
            value = -drop[(p - low) * N : (p - low + 1) * N, :]
            if q < 0:
                if p < 4:
                    value = value + flux(owner[p], side[p])
                else:
                    value = value + jnp.where(g_up, flux(1, 3), flux(0, 2))
            elif p < 4 and q < 4:
                if owner[p] == owner[q]:
                    value = value + entry(owner[p], side[p], side[q])
            elif p < 4:
                part = entry(owner[p], side[p], other[owner[p]])
                value = value + jnp.where(g_up if owner[p] == 1 else jnp.logical_not(g_up), part, 0.0)
            elif q < 4:
                part = entry(owner[q], other[owner[q]], side[q])
                value = value + jnp.where(g_up if owner[q] == 1 else jnp.logical_not(g_up), part, 0.0)
            else:
                value = value + jnp.where(g_up, entry(1, 3, 3), entry(0, 2, 2))
            ref, i = home[(p, q)]
            ref[i] = value


def pair_0(own, got, x_out, v_ref):
    x_out[...] = own[0] + got[0]
    invert(x_out, v_ref)


def pair_1(x11, own, got, x_out, x22, v_ref):
    s = own[0] + got[0]
    t = mm(s, x11[...])
    x22[...] = own[1] + got[1] - mm_nt(t, s)
    invert(x22, v_ref)
    low = mm(x22[...], t)
    x_out[N:, N:] = x22[...]
    x_out[N:, :N] = -low
    x_out[:N, N:] = -mm_tn(t, x22[...])
    x_out[:N, :N] = x11[...] + mm_tn(t, low)


def load(table, t):
    ref, i = table[t]
    return ref[i]


def merge1(x, own, got, face0, face1, a_ref):
    for q in range(2):
        cols = slice(q * N, (q + 1) * N)
        a_ref[0:N, cols] = own[q]
        a_ref[N:, cols] = got[q]
    yt = mm(a_ref[...], x[...])
    drop = mm_nt(yt, a_ref[0:N, :])
    face0[0] = own[2] - drop[:N]
    face1[0] = -drop[N:]
    face1[1] = got[2] - mm_nt(yt[N:], a_ref[N:, :])


def merge1_rest(x, own, own_flux, kept, got, got_flux, half0, half1, send, yt_ref, f_ref, a_ref):
    core = roles()[2]
    mine = put((SENT1, FLUX1, KEPT1), (own, own_flux, kept))
    theirs = put((SENT1, FLUX1), (got, got_flux))
    for q in range(2):
        cols = slice(q * N, (q + 1) * N)
        a_ref[0:N, cols] = load(mine, (4, q))
        a_ref[N : 2 * N, cols] = load(theirs, (4, q))
        a_ref[2 * N : 3 * N, cols] = load(mine, (2, q))
        a_ref[3 * N : 4 * N, cols] = load(mine, (3, q))
        f_ref[cols, :] = load(mine, (q, -1)) + load(theirs, (q, -1))
    yt_ref[...] = mm(a_ref[...], x[...])
    base = {
        (2, 0): (mine, (2, 4)), (3, 0): (mine, (3, 4)),
        (2, 2): (mine, (2, 2)), (3, 2): (mine, (3, 2)), (3, 3): (mine, (3, 3)),
        (0, -1): (mine, (4, -1)), (1, -1): (theirs, (4, -1)), (2, -1): (mine, (2, -1)), (3, -1): (mine, (3, -1)),
    }
    spread(((0, 2), (1, 2), (2, 2), (3, 3), (-1, 0)), HALF2, (half0, half1), base, load, yt_ref, a_ref, f_ref)
    half1[5] = jnp.zeros((N, N), F32)
    pick_half(core, half0, half1, send)


def spread(spans, batches, refs, base, take, yt, a_ref, f_ref):
    home = put(batches, refs)
    for q, low in spans:
        if q < 0:
            drop = mm(yt[...], f_ref[...])
        else:
            drop = mm_nt(yt[low * N :, :], a_ref[q * N : (q + 1) * N, :])
        for p in range(low, 4):
            value = -drop[(p - low) * N : (p - low + 1) * N, :]
            if (p, q) in base:
                value = value + take(*base[(p, q)])
            ref, i = home[(p, q)]
            ref[i] = value


def pick_half(core, half0, half1, send):
    @pl.when(core == 0)
    def _():
        send[...] = half0[...]

    @pl.when(core == 1)
    def _():
        send[...] = half1[...]


def sides2(half0, half1, got, swapped):
    core, b1 = roles()[2:]
    table = put(HALF2, (half0, half1))
    which = {t: h for h in range(2) for t in HALF2[h]}

    def mate(t):
        i = table[t][1]
        return jnp.where(core == which[t], got[i], swapped[i])

    def of(half, t):
        return jnp.where(b1 == half, load(table, t), mate(t))

    def both(t):
        return load(table, t) + mate(t)

    return of, both


def merge2(x, half0, half1, got, swapped, sent0, sent1, half3, half4, send, yt_ref, f_ref, a_ref):
    of, both = sides2(half0, half1, got, swapped)
    for q in range(2):
        cols = slice(q * N, (q + 1) * N)
        for p in range(4):
            a_ref[p * N : (p + 1) * N, cols] = of(p // 2, (2 + p % 2, q))
        f_ref[cols, :] = both((q, -1))
    yt_ref[...] = mm(a_ref[...], x[...])
    base = {(p, q): (p // 2, (2 + p % 2, 2 + q % 2)) for p in range(4) for q in range(p + 1) if p // 2 == q // 2}
    base.update({(p, -1): (p // 2, (2 + p % 2, -1)) for p in range(4)})
    spans = ((0, 0), (1, 1), (2, 2), (3, 3), (-1, 0))
    spread(spans, SENT3 + HALF3, (sent0, sent1, half3, half4), base, of, yt_ref, a_ref, f_ref)
    pick_half(roles()[2], half3, half4, send)


def solve_1(x0, own, got, s10, low10, x_out, v_ref):
    s = own[0] + got[0]
    low = mm(s, x0[...])
    s10[...] = s
    low10[...] = low
    x_out[...] = own[1] + got[1] - mm_nt(low, s)
    invert(x_out, v_ref)


def solve_2(x0, x1, s10, own, got, s20, l20, s21, l21, x_out, v_ref):
    s = own[2] + got[2]
    low = mm(s, x0[...])
    s20[...], l20[...] = s, low
    t = own[3] + got[3] - mm_nt(low, s10[...])
    u = mm(t, x1[...])
    s21[...], l21[...] = t, u
    x_out[...] = own[4] + got[4] - mm_nt(low, s) - mm_nt(u, t)
    invert(x_out, v_ref)


def solve_3(x0, x1, x2, s10, low10, s20, l20, s21, l21, half3, half4, got, swapped, xx2, yt2, f2, xx1, yt1, f1,
            kept, send, x3, v_ref, u, v):
    _, _, core, b1 = roles()

    def mate(h, i):
        return jnp.where(core == h, got[i], swapped[i])

    s30 = half3[0] + mate(0, 0)
    l30 = mm(s30, x0[...])
    s31 = half3[1] + mate(0, 1) - mm_nt(l30, s10[...])
    l31 = mm(s31, x1[...])
    s32 = half3[2] + mate(0, 2) - mm_nt(l30, s20[...]) - mm_nt(l31, s21[...])
    l32 = mm(s32, x2[...])
    x3[...] = half3[3] + mate(0, 3) - mm_nt(l30, s30) - mm_nt(l31, s31) - mm_nt(l32, s32)
    own2, own1 = mm(xx2[...], f2[...]), mm(xx1[...], f1[...])
    invert(x3, v_ref)
    f = [half4[i] + mate(1, i) for i in range(4)]
    f[1] = f[1] - mm(low10[...], f[0])
    f[2] = f[2] - mm(l20[...], f[0]) - mm(l21[...], f[1])
    f[3] = f[3] - mm(l30, f[0]) - mm(l31, f[1]) - mm(l32, f[2])
    p2, p1, p0 = mm(x2[...], f[2]), mm(x1[...], f[1]), mm(x0[...], f[0])
    w3 = mm(x3[...], f[3])
    w2 = p2 - mm_tn(l32, w3)
    w1 = p1 - mm_tn(l31, w3) - mm_tn(l21[...], w2)
    w0 = p0 - mm_tn(l30, w3) - mm_tn(l20[...], w2) - mm_tn(low10[...], w1)
    for i, w in enumerate((w0, w1, w2, w3)):
        u[i * N : (i + 1) * N, :] = -w
    face2 = -(mm_tn(yt2[...], u[...]) + own2)
    v[: 2 * N, :] = face2
    v[2 * N :, :] = jnp.where(b1 == 0, u[: 2 * N, :], u[2 * N :, :])
    face1 = -(mm_tn(yt1[...], v[...]) + own1)
    kept[: 2 * N, :] = face1
    kept[2 * N : 4 * N, :] = v[2 * N :, :]
    kept[4 * N :, :] = face2[:N, :]
    send[: 2 * N, :] = face1
    send[2 * N :, :] = face2[N:, :]


def descend(kept, got, y0, w0, out):
    a0, a1, b0, b1 = roles()
    inner = (a0 ^ a1) == 1
    face1 = jnp.where(inner, kept[: 2 * N, :], got[: 2 * N, :])
    side_h = jnp.where(inner, kept[2 * N : 4 * N, :], 0.0)
    side_g = jnp.where(inner, kept[4 * N :, :], got[2 * N :, :])
    face0 = -(mm(y0[...], jnp.concatenate([face1, side_h, side_g], axis=0)) + w0[...])
    mine_1 = jnp.where(b0 == 0, face1[:N, :], face1[N:, :])
    mine_h = jnp.where(b0 == 0, side_h[:N, :], side_h[N:, :])
    mine_g = jnp.where((b0 ^ b1) == 1, side_g, 0.0)
    out[:N, :] = jnp.where(a0 == 0, mine_h, mine_1)
    out[N : 2 * N, :] = jnp.where(a0 == 0, mine_1, mine_h)
    out[2 * N : 3 * N, :] = jnp.where(b0 == 0, mine_g, face0)
    out[3 * N :, :] = jnp.where(b0 == 0, face0, mine_g)


def call(body, outs, scratch, weight, *args):
    vmem = pl.BlockSpec(memory_space=pltpu.VMEM)
    return pl.pallas_call(
        body,
        out_shape=tuple(jax.ShapeDtypeStruct(shape, F32) for shape in outs),
        in_specs=[vmem] * len(args),
        out_specs=tuple(vmem for _ in outs),
        scratch_shapes=[pltpu.VMEM(shape, F32) for shape in scratch],
        compiler_params=pltpu.CompilerParams(vmem_limit_bytes=12 * 2**20),
        cost_estimate=pl.CostEstimate(flops=weight * 10**9, bytes_accessed=weight * 10**6, transcendentals=0),
    )(*args)


def flip(block, axis, bit):
    count = lax.axis_size(axis)
    return lax.ppermute(block, axis, [(i, i ^ (1 << bit)) for i in range(count)])


def tiles(count):
    return (count, N, N)


def shards(leaf_maps, leaf_fluxes):
    own_map, own_flux = leaf_maps[0, 0], leaf_fluxes[0, 0]
    mate_map = flip(own_map, "gy", 0)
    mate_flux = flip(own_flux, "gy", 0)
    map_v, flux_v = call(fetch, [(4 * N, 4 * N), (4 * N, N)], [], 1, own_map, own_flux)
    count = lax.axis_size("gx")
    inward = [pair for i in range(0, count, 4) for pair in ((i, i + 1), (i + 3, i + 2))]
    outward = [(b, a) for a, b in inward]
    inner = [pair for i in range(1, count, 4) for pair in ((i, i + 1), (i + 1, i))]
    square, wide = (N, N), (4 * N, 2 * N)

    x0, face, face_b = call(merge0, [square, tiles(1), tiles(2)], [square], 6, map_v, mate_map)
    got_a = lax.ppermute(face, "gx", inward)
    got_b = lax.ppermute(face_b, "gx", inward)
    sent1, flux1, kept1, y0, w0 = call(
        merge0_rest, [tiles(3), tiles(3), tiles(len(KEPT1)), (N, 5 * N), square], [(N, 6 * N), (5 * N, N)], 2,
        map_v, flux_v, mate_map, mate_flux, x0,
    )
    got_c = lax.ppermute(sent1, "gx", inward)
    got_d = lax.ppermute(flux1, "gx", inward)
    (xa,) = call(pair_0, [square], [square], 6, face, got_a)
    (x1,) = call(pair_1, [(2 * N, 2 * N)], [square, square], 6, xa, face_b, got_b)

    face, face_b = call(merge1, [tiles(1), tiles(2)], [(2 * N, 2 * N)], 1, x1, sent1, got_c)
    got_a = flip(face, "gy", 1)
    got_b = flip(face_b, "gy", 1)
    h2a, h2b, sent2, yt1, f1 = call(
        merge1_rest, [tiles(6), tiles(6), tiles(6), wide, (2 * N, N)], [wide], 2,
        x1, sent1, flux1, kept1, got_c, got_d,
    )
    got_c = flip(sent2, "gy", 1)
    (xa,) = call(pair_0, [square], [square], 6, face, got_a)
    (x2,) = call(pair_1, [(2 * N, 2 * N)], [square, square], 6, xa, face_b, got_b)
    got_d = flip(got_c, "gy", 0)

    face, s3b, h3a, h3b, sent3, yt2, f2 = call(
        merge2, [tiles(1), tiles(5), tiles(4), tiles(4), tiles(4), wide, (2 * N, N)], [wide], 2,
        x2, h2a, h2b, got_c, got_d,
    )
    got_a = lax.ppermute(face, "gx", inner)
    got_b = lax.ppermute(s3b, "gx", inner)
    (z0,) = call(pair_0, [square], [square], 6, face, got_a)
    got_c = lax.ppermute(sent3, "gx", inner)
    s10, low10, z1 = call(solve_1, [square] * 3, [square], 6, z0, s3b, got_b)
    s20, l20, s21, l21, z2 = call(solve_2, [square] * 5, [square], 7, z0, z1, s10, s3b, got_b)
    got_d = flip(got_c, "gy", 0)
    kept, send = call(
        solve_3, [(5 * N, N), (3 * N, N)], [square, square, (4 * N, N), (4 * N, N)], 10,
        z0, z1, z2, s10, low10, s20, l20, s21, l21, h3a, h3b, got_c, got_d, x2, yt2, f2, x1, yt1, f1,
    )
    down = lax.ppermute(send, "gx", outward)
    (out,) = call(descend, [(4 * N, N)], [], 1, kept, down, y0, w0)
    return out[None, None]


def solution(mesh):
    spec = P("gx", "gy", None, None)

    return jax.shard_map(shards, mesh=mesh, in_specs=(spec, spec), out_specs=spec, check_vma=False)
```

```python
import jax
import jax.numpy as jnp
from jax import lax
from jax.experimental import pallas as pl
from jax.experimental.pallas import tpu as pltpu
from jax.sharding import PartitionSpec as P


N = 128
F32 = jnp.float32

SENT1 = ((4, 0), (4, 1), (4, 4))
FLUX1 = ((0, -1), (1, -1), (4, -1))
KEPT1 = ((2, 0), (2, 1), (3, 0), (3, 1), (2, 2), (3, 2), (3, 3), (2, 4), (3, 4), (2, -1), (3, -1))
HALF2 = (((2, 0), (2, 1), (3, 0), (3, 1), (0, -1), (1, -1)), ((2, 2), (3, 2), (3, 3), (2, -1), (3, -1)))
SENT3 = (((0, 0), (1, 0), (1, 1)),)
HALF3 = (
    ((2, 0), (2, 1), (2, 2), (3, 0), (3, 1), (3, 2), (3, 3)),
    ((2, 0), (2, 1), (2, 2), (0, -1), (1, -1), (2, -1), (3, -1)),
)


def put(batches, refs):
    return {t: (ref, i) for batch, ref in zip(batches, refs) for i, t in enumerate(batch)}


def roles():
    col = lax.axis_index("gx")
    row = lax.axis_index("gy")
    return col & 1, (col >> 1) & 1, row & 1, (row >> 1) & 1


def halves(x):
    top = x.astype(jnp.bfloat16)
    return top, (x - top.astype(F32)).astype(jnp.bfloat16)


def triple(x, y, dims):
    xh, xl = halves(x)
    yh, yl = halves(y)

    def dot(p, q):
        return lax.dot_general(p, q, (dims, ((), ())), preferred_element_type=F32)

    return dot(xh, yh) + (dot(xh, yl) + dot(xl, yh))


def mm(x, y):
    return triple(x, y, ((1,), (0,)))


def mm_nt(x, y):
    return triple(x, y, ((1,), (1,)))


def mm_tn(x, y):
    return triple(x, y, ((0,), (0,)))


def over(x, rows=8):
    return jnp.broadcast_to(x, (rows, N))


def invert(x_ref, v_ref):
    lane = lax.broadcasted_iota(jnp.int32, (8, N), 1)
    sub = lax.broadcasted_iota(jnp.int32, (8, N), 0)
    rows = [x_ref[8 * i : 8 * i + 8, :] for i in range(N // 8)]
    for j in range(N // 8):
        top = rows[j]
        inside = (lane >= 8 * j) & (lane < 8 * j + 8)
        seed = jnp.where(inside, jnp.where(lane - 8 * j == sub, 1.0, 0.0), top)
        cols = {c: over(top[:, 8 * j + c : 8 * j + c + 1]) for c in range(8)}
        panel = seed
        for k in range(0, 8, 2):
            a, b = over(cols[k][k : k + 1, :]), over(cols[k + 1][k : k + 1, :])
            d = over(cols[k + 1][k + 1 : k + 2, :])
            recip = 1.0 / (a * d - b * b)

            def pivot(x, k=k, cols=cols, a=a, b=b, d=d, recip=recip):
                t0, t1 = over(x[k : k + 1, :]), over(x[k + 1 : k + 2, :])
                s0, s1 = d * t0 - b * t1, a * t1 - b * t0
                pure = x - (cols[k] * s0 + cols[k + 1] * s1) * recip
                return jnp.where(sub == k, s0 * recip, jnp.where(sub == k + 1, s1 * recip, pure))

            panel = pivot(panel)
            cols = {c: pivot(cols[c]) for c in range(k + 2, 8)}
        low = lane < 8 * j + 8
        v_ref[8 * j : 8 * j + 8, :] = jnp.where(low, seed, 0.0)
        x_ref[8 * j : 8 * j + 8, :] = jnp.where(low, panel, 0.0)
        lines = [over(panel[k : k + 1, :]) for k in range(8)]
        for i in range(j + 1, N // 8):
            b = [over(rows[i][:, 8 * j + k : 8 * j + k + 1]) * lines[k] for k in range(8)]
            total = ((b[0] + b[1]) + (b[2] + b[3])) + ((b[4] + b[5]) + (b[6] + b[7]))
            rows[i] = jnp.where(inside, 0.0, rows[i]) - total
    x_ref[...] = mm_tn(v_ref[...], x_ref[...])


class Leaves:
    def __init__(self, own_map, mate_map, own_flux=None, mate_flux=None):
        a0, _, b0, b1 = roles()
        self.maps, self.fluxes = (own_map, mate_map), (own_flux, mate_flux)
        self.mine_low, self.g_up = b0 == 0, b1 == 0
        self.f1, self.h = 1 - a0, a0

    def pick(self, leaf, mine, mate):
        return jnp.where(self.mine_low, mine, mate) if leaf == 0 else jnp.where(self.mine_low, mate, mine)

    def entry(self, leaf, r, c):
        return self.pick(leaf, *(ref[at(r), at(c)] for ref in self.maps))

    def flux(self, leaf, r):
        return self.pick(leaf, *(ref[at(r), :] for ref in self.fluxes))


def at(side):
    return pl.ds(side * N, N) if isinstance(side, int) else pl.ds(pl.multiple_of(side * N, N), N)


def fetch(own_map, own_flux, map_out, flux_out):
    map_out[...] = own_map[...]
    flux_out[...] = own_flux[...]


def merge0(map_out, mate_map, x_ref, face0, face1, v_ref):
    a0, _, b0, _ = roles()
    low = b0 == 0
    f1, mine, his = 1 - a0, 3 - b0, 2 + b0
    x_ref[...] = map_out[at(mine), at(mine)] + mate_map[at(his), at(his)]
    invert(x_ref, v_ref)
    ours = (map_out[at(mine), at(f1)], map_out[at(f1), at(mine)], map_out[at(f1), at(f1)])
    theirs = (mate_map[at(his), at(f1)], mate_map[at(f1), at(his)], mate_map[at(f1), at(f1)])
    lower = [jnp.where(low, o, t) for o, t in zip(ours, theirs)]
    upper = [jnp.where(low, t, o) for o, t in zip(ours, theirs)]
    y_low, y_up = mm(x_ref[...], lower[0]), mm(x_ref[...], upper[0])
    face0[0] = lower[2] - mm(lower[1], y_low)
    face1[0] = -mm(upper[1], y_low)
    face1[1] = upper[2] - mm(upper[1], y_up)


def merge0_rest(own_map, own_flux, mate_map, mate_flux, x_ref, sent, flux_sent, kept, y_ref, w_ref, rhs, rows):
    leaves = Leaves(own_map, mate_map, own_flux, mate_flux)
    entry, flux, g_up = leaves.entry, leaves.flux, leaves.g_up
    face, other = (3, 2), (2, 3)
    owner = (0, 1, 0, 1)
    side = (leaves.f1, leaves.f1, leaves.h, leaves.h)
    for p in range(4):
        rhs[:, p * N : (p + 1) * N] = entry(owner[p], face[owner[p]], side[p])
        rows[p * N : (p + 1) * N, :] = entry(owner[p], side[p], face[owner[p]])
    rhs[:, 4 * N : 5 * N] = jnp.where(g_up, entry(1, 2, 3), entry(0, 3, 2))
    rows[4 * N : 5 * N, :] = jnp.where(g_up, entry(1, 3, 2), entry(0, 2, 3))
    rhs[:, 5 * N : 6 * N] = flux(0, 3) + flux(1, 2)
    out = mm(x_ref[...], rhs[...])
    y_ref[...] = out[:, : 5 * N]
    w_ref[...] = out[:, 5 * N :]
    home = put((SENT1, FLUX1, KEPT1), (sent, flux_sent, kept))
    for q, low, high in ((0, 2, 5), (1, 2, 5), (2, 2, 4), (3, 3, 4), (4, 2, 5), (-1, 0, 5)):
        cq = 5 if q < 0 else q
        drop = mm(rows[low * N : high * N, :], out[:, cq * N : (cq + 1) * N])
        for p in range(low, high):
            value = -drop[(p - low) * N : (p - low + 1) * N, :]
            if q < 0:
                if p < 4:
                    value = value + flux(owner[p], side[p])
                else:
                    value = value + jnp.where(g_up, flux(1, 3), flux(0, 2))
            elif p < 4 and q < 4:
                if owner[p] == owner[q]:
                    value = value + entry(owner[p], side[p], side[q])
            elif p < 4:
                part = entry(owner[p], side[p], other[owner[p]])
                value = value + jnp.where(g_up if owner[p] == 1 else jnp.logical_not(g_up), part, 0.0)
            elif q < 4:
                part = entry(owner[q], other[owner[q]], side[q])
                value = value + jnp.where(g_up if owner[q] == 1 else jnp.logical_not(g_up), part, 0.0)
            else:
                value = value + jnp.where(g_up, entry(1, 3, 3), entry(0, 2, 2))
            ref, i = home[(p, q)]
            ref[i] = value


def pair_0(own, got, x_out, v_ref):
    x_out[...] = own[0] + got[0]
    invert(x_out, v_ref)


def pair_1(x11, own, got, x_out, x22, v_ref):
    s = own[0] + got[0]
    t = mm(s, x11[...])
    x22[...] = own[1] + got[1] - mm_nt(t, s)
    invert(x22, v_ref)
    low = mm(x22[...], t)
    x_out[N:, N:] = x22[...]
    x_out[N:, :N] = -low
    x_out[:N, N:] = -mm_tn(t, x22[...])
    x_out[:N, :N] = x11[...] + mm_tn(t, low)


def load(table, t):
    ref, i = table[t]
    return ref[i]


def merge1(x, own, got, face0, face1, a_ref):
    for q in range(2):
        cols = slice(q * N, (q + 1) * N)
        a_ref[0:N, cols] = own[q]
        a_ref[N:, cols] = got[q]
    yt = mm(a_ref[...], x[...])
    drop = mm_nt(yt, a_ref[0:N, :])
    face0[0] = own[2] - drop[:N]
    face1[0] = -drop[N:]
    face1[1] = got[2] - mm_nt(yt[N:], a_ref[N:, :])


def merge1_rest(x, own, own_flux, kept, got, got_flux, half0, half1, send, yt_ref, f_ref, a_ref):
    core = roles()[2]
    mine = put((SENT1, FLUX1, KEPT1), (own, own_flux, kept))
    theirs = put((SENT1, FLUX1), (got, got_flux))
    for q in range(2):
        cols = slice(q * N, (q + 1) * N)
        a_ref[0:N, cols] = load(mine, (4, q))
        a_ref[N : 2 * N, cols] = load(theirs, (4, q))
        a_ref[2 * N : 3 * N, cols] = load(mine, (2, q))
        a_ref[3 * N : 4 * N, cols] = load(mine, (3, q))
        f_ref[cols, :] = load(mine, (q, -1)) + load(theirs, (q, -1))
    yt_ref[...] = mm(a_ref[...], x[...])
    base = {
        (2, 0): (mine, (2, 4)), (3, 0): (mine, (3, 4)),
        (2, 2): (mine, (2, 2)), (3, 2): (mine, (3, 2)), (3, 3): (mine, (3, 3)),
        (0, -1): (mine, (4, -1)), (1, -1): (theirs, (4, -1)), (2, -1): (mine, (2, -1)), (3, -1): (mine, (3, -1)),
    }
    spread(((0, 2), (1, 2), (2, 2), (3, 3), (-1, 0)), HALF2, (half0, half1), base, load, yt_ref, a_ref, f_ref)
    half1[5] = jnp.zeros((N, N), F32)
    pick_half(core, half0, half1, send)


def spread(spans, batches, refs, base, take, yt, a_ref, f_ref):
    for q, low in spans:
        if q < 0:
            drop = mm(yt[...], f_ref[...])
        else:
            drop = mm_nt(yt[low * N :, :], a_ref[q * N : (q + 1) * N, :])
        for p in range(low, 4):
            value = -drop[(p - low) * N : (p - low + 1) * N, :]
            if (p, q) in base:
                value = value + take(*base[(p, q)])
            for batch, ref in zip(batches, refs):
                if (p, q) in batch:
                    ref[batch.index((p, q))] = value


def pick_half(core, half0, half1, send):
    @pl.when(core == 0)
    def _():
        send[...] = half0[...]

    @pl.when(core == 1)
    def _():
        send[...] = half1[...]


def sides2(half0, half1, got, swapped):
    core, b1 = roles()[2:]
    table = put(HALF2, (half0, half1))
    which = {t: h for h in range(2) for t in HALF2[h]}

    def mate(t):
        i = table[t][1]
        return jnp.where(core == which[t], got[i], swapped[i])

    def of(half, t):
        return jnp.where(b1 == half, load(table, t), mate(t))

    def both(t):
        return load(table, t) + mate(t)

    return of, both


def merge2(x, half0, half1, got, swapped, sent0, half3, half4, send, yt_ref, f_ref, a_ref):
    of, both = sides2(half0, half1, got, swapped)
    for q in range(2):
        cols = slice(q * N, (q + 1) * N)
        for p in range(4):
            a_ref[p * N : (p + 1) * N, cols] = of(p // 2, (2 + p % 2, q))
        f_ref[cols, :] = both((q, -1))
    yt_ref[...] = mm(a_ref[...], x[...])
    base = {(p, q): (p // 2, (2 + p % 2, 2 + q % 2)) for p in range(4) for q in range(p + 1) if p // 2 == q // 2}
    base.update({(p, -1): (p // 2, (2 + p % 2, -1)) for p in range(4)})
    spans = ((0, 0), (1, 1), (2, 2), (3, 3), (-1, 0))
    spread(spans, SENT3 + HALF3, (sent0, half3, half4), base, of, yt_ref, a_ref, f_ref)
    pick_half(roles()[2], half3, half4, send)


def solve_low(own, got, x0, x1, s10, low10, v_ref, xs):
    xs[0] = own[0] + got[0]
    s10[...] = own[1] + got[1]
    xs[1] = own[2] + got[2]

    def step(i, carry):
        invert(xs.at[i], v_ref)

        @pl.when(i == 0)
        def _():
            low10[...] = mm(s10[...], xs[0])
            xs[1] = xs[1] - mm_nt(low10[...], s10[...])

        return carry

    lax.fori_loop(0, 2, step, 0)
    x0[...] = xs[0]
    x1[...] = xs[1]


def solve_2(x0, x1, s10, half3, got, s20, l20, s21, l21, x_out, v_ref):
    s = half3[0] + got[0]
    low = mm(s, x0[...])
    s20[...], l20[...] = s, low
    t = half3[1] + got[1] - mm_nt(low, s10[...])
    u = mm(t, x1[...])
    s21[...], l21[...] = t, u
    x_out[...] = half3[2] + got[2] - mm_nt(low, s) - mm_nt(u, t)
    invert(x_out, v_ref)


def solve_3(x0, x1, x2, s10, low10, s20, l20, s21, l21, half3, half4, got, swapped, xx2, yt2, f2, xx1, yt1, f1,
            kept, send, x3, v_ref):
    _, _, core, b1 = roles()

    def mate(h, i):
        return jnp.where(core == h, got[i], swapped[i])

    s30 = half3[3] + mate(0, 3)
    l30 = mm(s30, x0[...])
    s31 = half3[4] + mate(0, 4) - mm_nt(l30, s10[...])
    l31 = mm(s31, x1[...])
    s32 = half3[5] + mate(0, 5) - mm_nt(l30, s20[...]) - mm_nt(l31, s21[...])
    l32 = mm(s32, x2[...])
    x3[...] = half3[6] + mate(0, 6) - mm_nt(l30, s30) - mm_nt(l31, s31) - mm_nt(l32, s32)
    invert(x3, v_ref)
    f = [half4[3 + i] + mate(1, 3 + i) for i in range(4)]
    f[1] = f[1] - mm(low10[...], f[0])
    f[2] = f[2] - mm(l20[...], f[0]) - mm(l21[...], f[1])
    f[3] = f[3] - mm(l30, f[0]) - mm(l31, f[1]) - mm(l32, f[2])
    p2 = mm(x2[...], f[2])
    p1 = mm(x1[...], f[1]) - mm_tn(l21[...], p2)
    p0 = mm(x0[...], f[0]) - mm_tn(l20[...], p2) - mm_tn(low10[...], p1)
    q2 = -l32
    q1 = -l31 - mm(q2, l21[...])
    q0 = -l30 - mm(q2, l20[...]) - mm(q1, low10[...])
    p = jnp.concatenate([p0, p1, p2], axis=0)
    q = jnp.concatenate([q0, q1, q2], axis=1)
    c2 = mm_tn(yt2[: 3 * N, :], p) - mm(xx2[...], f2[...])
    r2 = mm(q, yt2[: 3 * N, :]) + yt2[3 * N :, :]
    unit = jnp.where(
        lax.broadcasted_iota(jnp.int32, (N, N), 0) == lax.broadcasted_iota(jnp.int32, (N, N), 1), 1.0, 0.0
    )
    below = b1 == 0
    ph = jnp.where(below, p[: 2 * N], jnp.concatenate([p2, jnp.zeros((N, N), F32)], axis=0))
    qh = jnp.where(below, q[:, : 2 * N], jnp.concatenate([q2, unit], axis=1))
    c1 = mm_tn(yt1[2 * N :, :], ph) - mm_tn(yt1[: 2 * N, :], c2) - mm(xx1[...], f1[...])
    r1 = mm(qh, yt1[2 * N :, :]) - mm(r2, yt1[: 2 * N, :])
    w3 = mm(x3[...], f[3])
    tail = mm_tn(jnp.concatenate([r1, qh, r2], axis=1), w3)
    face1 = c1 + tail[: 2 * N]
    face2 = c2 + tail[4 * N :]
    kept[: 2 * N, :] = face1
    kept[2 * N : 4 * N, :] = -(ph + tail[2 * N : 4 * N])
    kept[4 * N :, :] = face2[:N]
    send[: 2 * N, :] = face1
    send[2 * N :, :] = face2[N:]


def descend(kept, got, y0, w0, out):
    a0, a1, b0, b1 = roles()
    inner = (a0 ^ a1) == 1
    face1 = jnp.where(inner, kept[: 2 * N, :], got[: 2 * N, :])
    side_h = jnp.where(inner, kept[2 * N : 4 * N, :], 0.0)
    side_g = jnp.where(inner, kept[4 * N :, :], got[2 * N :, :])
    face0 = -(mm(y0[...], jnp.concatenate([face1, side_h, side_g], axis=0)) + w0[...])
    mine_1 = jnp.where(b0 == 0, face1[:N, :], face1[N:, :])
    mine_h = jnp.where(b0 == 0, side_h[:N, :], side_h[N:, :])
    mine_g = jnp.where((b0 ^ b1) == 1, side_g, 0.0)
    out[:N, :] = jnp.where(a0 == 0, mine_h, mine_1)
    out[N : 2 * N, :] = jnp.where(a0 == 0, mine_1, mine_h)
    out[2 * N : 3 * N, :] = jnp.where(b0 == 0, mine_g, face0)
    out[3 * N :, :] = jnp.where(b0 == 0, face0, mine_g)


def call(body, outs, scratch, weight, *args):
    vmem = pl.BlockSpec(memory_space=pltpu.VMEM)
    return pl.pallas_call(
        body,
        out_shape=tuple(jax.ShapeDtypeStruct(shape, F32) for shape in outs),
        in_specs=[vmem] * len(args),
        out_specs=tuple(vmem for _ in outs),
        scratch_shapes=[pltpu.VMEM(shape, F32) for shape in scratch],
        compiler_params=pltpu.CompilerParams(vmem_limit_bytes=12 * 2**20),
        cost_estimate=pl.CostEstimate(flops=weight * 10**9, bytes_accessed=weight * 10**6, transcendentals=0),
    )(*args)


def flip(block, axis, bit):
    count = lax.axis_size(axis)
    return lax.ppermute(block, axis, [(i, i ^ (1 << bit)) for i in range(count)])


def tiles(count):
    return (count, N, N)


def shards(leaf_maps, leaf_fluxes):
    own_map, own_flux = leaf_maps[0, 0], leaf_fluxes[0, 0]
    mate_map = flip(own_map, "gy", 0)
    mate_flux = flip(own_flux, "gy", 0)
    map_v, flux_v = call(fetch, [(4 * N, 4 * N), (4 * N, N)], [], 1, own_map, own_flux)
    count = lax.axis_size("gx")
    inward = [pair for i in range(0, count, 4) for pair in ((i, i + 1), (i + 3, i + 2))]
    outward = [(b, a) for a, b in inward]
    inner = [pair for i in range(1, count, 4) for pair in ((i, i + 1), (i + 1, i))]
    square, wide = (N, N), (4 * N, 2 * N)

    x0, face, face_b = call(merge0, [square, tiles(1), tiles(2)], [square], 6, map_v, mate_map)
    got_a = lax.ppermute(face, "gx", inward)
    got_b = lax.ppermute(face_b, "gx", inward)
    sent1, flux1, kept1, y0, w0 = call(
        merge0_rest, [tiles(3), tiles(3), tiles(len(KEPT1)), (N, 5 * N), square], [(N, 6 * N), (5 * N, N)], 2,
        map_v, flux_v, mate_map, mate_flux, x0,
    )
    got_c = lax.ppermute(sent1, "gx", inward)
    got_d = lax.ppermute(flux1, "gx", inward)
    (xa,) = call(pair_0, [square], [square], 6, face, got_a)
    (x1,) = call(pair_1, [(2 * N, 2 * N)], [square, square], 6, xa, face_b, got_b)

    face, face_b = call(merge1, [tiles(1), tiles(2)], [(2 * N, 2 * N)], 1, x1, sent1, got_c)
    got_a = flip(face, "gy", 1)
    got_b = flip(face_b, "gy", 1)
    h2a, h2b, sent2, yt1, f1 = call(
        merge1_rest, [tiles(6), tiles(6), tiles(6), wide, (2 * N, N)], [wide], 2,
        x1, sent1, flux1, kept1, got_c, got_d,
    )
    got_c = flip(sent2, "gy", 1)
    (xa,) = call(pair_0, [square], [square], 6, face, got_a)
    (x2,) = call(pair_1, [(2 * N, 2 * N)], [square, square], 6, xa, face_b, got_b)
    got_d = flip(got_c, "gy", 0)

    low3, h3a, h3b, sent3, yt2, f2 = call(
        merge2, [tiles(3), tiles(7), tiles(7), tiles(7), wide, (2 * N, N)], [wide], 2,
        x2, h2a, h2b, got_c, got_d,
    )
    got_a = lax.ppermute(low3, "gx", inner)
    got_b = lax.ppermute(sent3, "gx", inner)
    z0, z1, s10, low10 = call(solve_low, [square] * 4, [square, tiles(2)], 12, low3, got_a)
    got_c = flip(got_b, "gy", 0)
    s20, l20, s21, l21, z2 = call(solve_2, [square] * 5, [square], 7, z0, z1, s10, h3a, got_b)
    kept, send = call(
        solve_3, [(5 * N, N), (3 * N, N)], [square, square], 10,
        z0, z1, z2, s10, low10, s20, l20, s21, l21, h3a, h3b, got_b, got_c, x2, yt2, f2, x1, yt1, f1,
    )
    down = lax.ppermute(send, "gx", outward)
    (out,) = call(descend, [(4 * N, N)], [], 1, kept, down, y0, w0)
    return out[None, None]


def solution(mesh):
    spec = P("gx", "gy", None, None)

    return jax.shard_map(shards, mesh=mesh, in_specs=(spec, spec), out_specs=spec, check_vma=False)
```

```python
import jax
import jax.numpy as jnp
from jax import lax
from jax.experimental import pallas as pl
from jax.experimental.pallas import tpu as pltpu
from jax.sharding import PartitionSpec as P


N = 128
F32 = jnp.float32

SENT1 = ((4, 0), (4, 1), (4, 4))
FLUX1 = ((0, -1), (1, -1), (4, -1))
KEPT1 = ((2, 0), (2, 1), (3, 0), (3, 1), (2, 2), (3, 2), (3, 3), (2, 4), (3, 4), (2, -1), (3, -1))
HALF2 = (((2, 0), (2, 1), (3, 0), (3, 1)), ((2, 2), (3, 2), (3, 3)))
FLUX2 = ((0, -1), (1, -1), (2, -1), (3, -1))
SENT3 = (((0, 0), (1, 0), (1, 1)),)
ROWS3 = ((2, 0), (2, 1), (2, 2), (3, 0), (3, 1), (3, 2), (3, 3))


def put(batches, refs):
    return {t: (ref, i) for batch, ref in zip(batches, refs) for i, t in enumerate(batch)}


def roles():
    col = lax.axis_index("gx")
    row = lax.axis_index("gy")
    return col & 1, (col >> 1) & 1, row & 1, (row >> 1) & 1


def halves(x):
    top = x.astype(jnp.bfloat16)
    return top, (x - top.astype(F32)).astype(jnp.bfloat16)


def triple(x, y, dims):
    xh, xl = halves(x)
    yh, yl = halves(y)

    def dot(p, q):
        return lax.dot_general(p, q, (dims, ((), ())), preferred_element_type=F32)

    return dot(xh, yh) + (dot(xh, yl) + dot(xl, yh))


def mm(x, y):
    return triple(x, y, ((1,), (0,)))


def mm_nt(x, y):
    return triple(x, y, ((1,), (1,)))


def mm_tn(x, y):
    return triple(x, y, ((0,), (0,)))


def over(x, rows=8):
    return jnp.broadcast_to(x, (rows, N))


def invert(x_ref, v_ref):
    lane = lax.broadcasted_iota(jnp.int32, (8, N), 1)
    sub = lax.broadcasted_iota(jnp.int32, (8, N), 0)
    rows = [x_ref[8 * i : 8 * i + 8, :] for i in range(N // 8)]
    for j in range(N // 8):
        top = rows[j]
        inside = (lane >= 8 * j) & (lane < 8 * j + 8)
        seed = jnp.where(inside, jnp.where(lane - 8 * j == sub, 1.0, 0.0), top)
        cols = {c: over(top[:, 8 * j + c : 8 * j + c + 1]) for c in range(8)}
        panel = seed
        for k in range(0, 8, 2):
            a, b = over(cols[k][k : k + 1, :]), over(cols[k + 1][k : k + 1, :])
            d = over(cols[k + 1][k + 1 : k + 2, :])
            recip = 1.0 / (a * d - b * b)

            def pivot(x, k=k, cols=cols, a=a, b=b, d=d, recip=recip):
                t0, t1 = over(x[k : k + 1, :]), over(x[k + 1 : k + 2, :])
                s0, s1 = d * t0 - b * t1, a * t1 - b * t0
                pure = x - (cols[k] * s0 + cols[k + 1] * s1) * recip
                return jnp.where(sub == k, s0 * recip, jnp.where(sub == k + 1, s1 * recip, pure))

            panel = pivot(panel)
            cols = {c: pivot(cols[c]) for c in range(k + 2, 8)}
        low = lane < 8 * j + 8
        v_ref[8 * j : 8 * j + 8, :] = jnp.where(low, seed, 0.0)
        x_ref[8 * j : 8 * j + 8, :] = jnp.where(low, panel, 0.0)
        lines = [over(panel[k : k + 1, :]) for k in range(8)]
        for i in range(j + 1, N // 8):
            b = [over(rows[i][:, 8 * j + k : 8 * j + k + 1]) * lines[k] for k in range(8)]
            total = ((b[0] + b[1]) + (b[2] + b[3])) + ((b[4] + b[5]) + (b[6] + b[7]))
            rows[i] = jnp.where(inside, 0.0, rows[i]) - total
    x_ref[...] = mm_tn(v_ref[...], x_ref[...])


class Leaves:
    def __init__(self, own_map, mate_map, own_flux=None, mate_flux=None):
        a0, _, b0, b1 = roles()
        self.maps, self.fluxes = (own_map, mate_map), (own_flux, mate_flux)
        self.mine_low, self.g_up = b0 == 0, b1 == 0
        self.f1, self.h = 1 - a0, a0

    def pick(self, leaf, mine, mate):
        return jnp.where(self.mine_low, mine, mate) if leaf == 0 else jnp.where(self.mine_low, mate, mine)

    def entry(self, leaf, r, c):
        return self.pick(leaf, *(ref[at(r), at(c)] for ref in self.maps))

    def flux(self, leaf, r):
        return self.pick(leaf, *(ref[at(r), :] for ref in self.fluxes))


def at(side):
    return pl.ds(side * N, N) if isinstance(side, int) else pl.ds(pl.multiple_of(side * N, N), N)


def fetch(own_map, own_flux, map_out, flux_out):
    map_out[...] = own_map[...]
    flux_out[...] = own_flux[...]


def merge0(map_out, mate_map, x_ref, face0, face1, v_ref):
    a0, _, b0, _ = roles()
    low = b0 == 0
    f1, mine, his = 1 - a0, 3 - b0, 2 + b0
    x_ref[...] = map_out[at(mine), at(mine)] + mate_map[at(his), at(his)]
    invert(x_ref, v_ref)
    ours = (map_out[at(mine), at(f1)], map_out[at(f1), at(mine)], map_out[at(f1), at(f1)])
    theirs = (mate_map[at(his), at(f1)], mate_map[at(f1), at(his)], mate_map[at(f1), at(f1)])
    lower = [jnp.where(low, o, t) for o, t in zip(ours, theirs)]
    upper = [jnp.where(low, t, o) for o, t in zip(ours, theirs)]
    y_low, y_up = mm(x_ref[...], lower[0]), mm(x_ref[...], upper[0])
    face0[0] = lower[2] - mm(lower[1], y_low)
    face1[0] = -mm(upper[1], y_low)
    face1[1] = upper[2] - mm(upper[1], y_up)


def merge0_rest(own_map, own_flux, mate_map, mate_flux, x_ref, sent, flux_sent, kept, y_ref, w_ref, rhs, rows):
    leaves = Leaves(own_map, mate_map, own_flux, mate_flux)
    entry, flux, g_up = leaves.entry, leaves.flux, leaves.g_up
    face, other = (3, 2), (2, 3)
    owner = (0, 1, 0, 1)
    side = (leaves.f1, leaves.f1, leaves.h, leaves.h)
    for p in range(4):
        rhs[:, p * N : (p + 1) * N] = entry(owner[p], face[owner[p]], side[p])
        rows[p * N : (p + 1) * N, :] = entry(owner[p], side[p], face[owner[p]])
    rhs[:, 4 * N : 5 * N] = jnp.where(g_up, entry(1, 2, 3), entry(0, 3, 2))
    rows[4 * N : 5 * N, :] = jnp.where(g_up, entry(1, 3, 2), entry(0, 2, 3))
    rhs[:, 5 * N : 6 * N] = flux(0, 3) + flux(1, 2)
    out = mm(x_ref[...], rhs[...])
    y_ref[...] = out[:, : 5 * N]
    w_ref[...] = out[:, 5 * N :]
    home = put((SENT1, FLUX1, KEPT1), (sent, flux_sent, kept))
    for q, low, high in ((0, 2, 5), (1, 2, 5), (2, 2, 4), (3, 3, 4), (4, 2, 5), (-1, 0, 5)):
        cq = 5 if q < 0 else q
        drop = mm(rows[low * N : high * N, :], out[:, cq * N : (cq + 1) * N])
        for p in range(low, high):
            value = -drop[(p - low) * N : (p - low + 1) * N, :]
            if q < 0:
                if p < 4:
                    value = value + flux(owner[p], side[p])
                else:
                    value = value + jnp.where(g_up, flux(1, 3), flux(0, 2))
            elif p < 4 and q < 4:
                if owner[p] == owner[q]:
                    value = value + entry(owner[p], side[p], side[q])
            elif p < 4:
                part = entry(owner[p], side[p], other[owner[p]])
                value = value + jnp.where(g_up if owner[p] == 1 else jnp.logical_not(g_up), part, 0.0)
            elif q < 4:
                part = entry(owner[q], other[owner[q]], side[q])
                value = value + jnp.where(g_up if owner[q] == 1 else jnp.logical_not(g_up), part, 0.0)
            else:
                value = value + jnp.where(g_up, entry(1, 3, 3), entry(0, 2, 2))
            ref, i = home[(p, q)]
            ref[i] = value


def pair_0(own, got, x_out, v_ref):
    x_out[...] = own[0] + got[0]
    invert(x_out, v_ref)


def pair_1(x11, own, got, x_out, x22, v_ref):
    s = own[0] + got[0]
    t = mm(s, x11[...])
    x22[...] = own[1] + got[1] - mm_nt(t, s)
    invert(x22, v_ref)
    low = mm(x22[...], t)
    x_out[N:, N:] = x22[...]
    x_out[N:, :N] = -low
    x_out[:N, N:] = -mm_tn(t, x22[...])
    x_out[:N, :N] = x11[...] + mm_tn(t, low)


def load(table, t):
    ref, i = table[t]
    return ref[i]


def merge1(x, own, got, face0, face1, a_ref):
    for q in range(2):
        cols = slice(q * N, (q + 1) * N)
        a_ref[0:N, cols] = own[q]
        a_ref[N:, cols] = got[q]
    yt = mm(a_ref[...], x[...])
    drop = mm_nt(yt, a_ref[0:N, :])
    face0[0] = own[2] - drop[:N]
    face1[0] = -drop[N:]
    face1[1] = got[2] - mm_nt(yt[N:], a_ref[N:, :])


def merge1_rest(x, own, own_flux, kept, got, got_flux, half0, half1, send, flux2, yt_ref, f_ref, a_ref):
    core = roles()[2]
    mine = put((SENT1, FLUX1, KEPT1), (own, own_flux, kept))
    theirs = put((SENT1, FLUX1), (got, got_flux))
    for q in range(2):
        cols = slice(q * N, (q + 1) * N)
        a_ref[0:N, cols] = load(mine, (4, q))
        a_ref[N : 2 * N, cols] = load(theirs, (4, q))
        a_ref[2 * N : 3 * N, cols] = load(mine, (2, q))
        a_ref[3 * N : 4 * N, cols] = load(mine, (3, q))
        f_ref[cols, :] = load(mine, (q, -1)) + load(theirs, (q, -1))
    yt_ref[...] = mm(a_ref[...], x[...])
    base = {
        (2, 0): (mine, (2, 4)), (3, 0): (mine, (3, 4)),
        (2, 2): (mine, (2, 2)), (3, 2): (mine, (3, 2)), (3, 3): (mine, (3, 3)),
        (0, -1): (mine, (4, -1)), (1, -1): (theirs, (4, -1)), (2, -1): (mine, (2, -1)), (3, -1): (mine, (3, -1)),
    }
    spread(((0, 2), (1, 2), (2, 2), (3, 3), (-1, 0)), HALF2 + (FLUX2,), (half0, half1, flux2), base, load, yt_ref, a_ref, f_ref)
    half1[3] = jnp.zeros((N, N), F32)
    pick_half(core, half0, half1, send)


def spread(spans, batches, refs, base, take, yt, a_ref, f_ref):
    for q, low in spans:
        if q < 0:
            drop = mm(yt[...], f_ref[...])
        else:
            drop = mm_nt(yt[low * N :, :], a_ref[q * N : (q + 1) * N, :])
        for p in range(low, 4):
            value = -drop[(p - low) * N : (p - low + 1) * N, :]
            if (p, q) in base:
                value = value + take(*base[(p, q)])
            for batch, ref in zip(batches, refs):
                if (p, q) in batch:
                    ref[batch.index((p, q))] = value


def pick_half(core, half0, half1, send):
    @pl.when(core == 0)
    def _():
        send[...] = half0[...]

    @pl.when(core == 1)
    def _():
        send[...] = half1[...]


def sides2(half0, half1, got, swapped):
    core, b1 = roles()[2:]
    table = put(HALF2, (half0, half1))
    which = {t: h for h in range(2) for t in HALF2[h]}

    def mate(t):
        i = table[t][1]
        return jnp.where(core == which[t], got[i], swapped[i])

    def of(half, t):
        return jnp.where(b1 == half, load(table, t), mate(t))

    return of


def merge2(x, half0, half1, got, swapped, sent0, rows3, yt_ref, a_ref):
    of = sides2(half0, half1, got, swapped)
    for q in range(2):
        for p in range(4):
            a_ref[p * N : (p + 1) * N, q * N : (q + 1) * N] = of(p // 2, (2 + p % 2, q))
    yt_ref[...] = mm(a_ref[...], x[...])
    base = {(p, q): (p // 2, (2 + p % 2, 2 + q % 2)) for p in range(4) for q in range(p + 1) if p // 2 == q // 2}
    spans = ((0, 0), (1, 1), (2, 2), (3, 3))
    spread(spans, SENT3 + (ROWS3,), (sent0, rows3), base, of, yt_ref, a_ref, None)


def merge2_flux(x2, x1, f1, yt2, own, got, rows3, f2, flux3, send, own2, own1):
    core, b1 = roles()[2:]
    f2[:N, :] = own[0] + got[0]
    f2[N:, :] = own[1] + got[1]
    drop = mm(yt2[...], f2[...])
    for p in range(4):
        value = jnp.where(b1 == p // 2, own[2 + p % 2], got[2 + p % 2])
        flux3[p] = value - drop[p * N : (p + 1) * N]
    send[:3] = rows3[:3]

    @pl.when(core == 0)
    def _():
        send[3:] = rows3[3:]

    @pl.when(core == 1)
    def _():
        send[3:] = flux3[...]

    own2[...] = mm(x2[...], f2[...])
    own1[...] = mm(x1[...], f1[...])


def solve_low(own, got, x0, x1, s10, low10, v_ref, xs):
    xs[0] = own[0] + got[0]
    s10[...] = own[1] + got[1]
    xs[1] = own[2] + got[2]

    def step(i, carry):
        invert(xs.at[i], v_ref)

        @pl.when(i == 0)
        def _():
            low10[...] = mm(s10[...], xs[0])
            xs[1] = xs[1] - mm_nt(low10[...], s10[...])

        return carry

    lax.fori_loop(0, 2, step, 0)
    x0[...] = xs[0]
    x1[...] = xs[1]


def solve_2(x0, x1, s10, half3, got, s20, l20, s21, l21, x_out, v_ref):
    s = half3[0] + got[0]
    low = mm(s, x0[...])
    s20[...], l20[...] = s, low
    t = half3[1] + got[1] - mm_nt(low, s10[...])
    u = mm(t, x1[...])
    s21[...], l21[...] = t, u
    x_out[...] = half3[2] + got[2] - mm_nt(low, s) - mm_nt(u, t)
    invert(x_out, v_ref)


def solve_3(x0, x1, x2, s10, low10, s20, l20, s21, l21, rows3, flux3, got, swapped, yt2, own2, yt1, own1,
            kept, send, x3, v_ref, u, v):
    _, _, core, b1 = roles()

    def mate(h, i):
        return jnp.where(core == h, got[i], swapped[i])

    s30 = rows3[3] + mate(0, 3)
    l30 = mm(s30, x0[...])
    s31 = rows3[4] + mate(0, 4) - mm_nt(l30, s10[...])
    l31 = mm(s31, x1[...])
    s32 = rows3[5] + mate(0, 5) - mm_nt(l30, s20[...]) - mm_nt(l31, s21[...])
    l32 = mm(s32, x2[...])
    x3[...] = rows3[6] + mate(0, 6) - mm_nt(l30, s30) - mm_nt(l31, s31) - mm_nt(l32, s32)
    invert(x3, v_ref)
    f = [flux3[i] + mate(1, 3 + i) for i in range(4)]
    f[1] = f[1] - mm(low10[...], f[0])
    f[2] = f[2] - mm(l20[...], f[0]) - mm(l21[...], f[1])
    f[3] = f[3] - mm(l30, f[0]) - mm(l31, f[1]) - mm(l32, f[2])
    p2, p1, p0 = mm(x2[...], f[2]), mm(x1[...], f[1]), mm(x0[...], f[0])
    w3 = mm(x3[...], f[3])
    w2 = p2 - mm_tn(l32, w3)
    w1 = p1 - mm_tn(l31, w3) - mm_tn(l21[...], w2)
    w0 = p0 - mm_tn(l30, w3) - mm_tn(l20[...], w2) - mm_tn(low10[...], w1)
    for i, w in enumerate((w0, w1, w2, w3)):
        u[i * N : (i + 1) * N, :] = -w
    face2 = -(mm_tn(yt2[...], u[...]) + own2[...])
    v[: 2 * N, :] = face2
    v[2 * N :, :] = jnp.where(b1 == 0, u[: 2 * N, :], u[2 * N :, :])
    face1 = -(mm_tn(yt1[...], v[...]) + own1[...])
    kept[: 2 * N, :] = face1
    kept[2 * N : 4 * N, :] = v[2 * N :, :]
    kept[4 * N :, :] = face2[:N, :]
    send[: 2 * N, :] = face1
    send[2 * N :, :] = face2[N:, :]


def descend(kept, got, y0, w0, out):
    a0, a1, b0, b1 = roles()
    inner = (a0 ^ a1) == 1
    face1 = jnp.where(inner, kept[: 2 * N, :], got[: 2 * N, :])
    side_h = jnp.where(inner, kept[2 * N : 4 * N, :], 0.0)
    side_g = jnp.where(inner, kept[4 * N :, :], got[2 * N :, :])
    face0 = -(mm(y0[...], jnp.concatenate([face1, side_h, side_g], axis=0)) + w0[...])
    mine_1 = jnp.where(b0 == 0, face1[:N, :], face1[N:, :])
    mine_h = jnp.where(b0 == 0, side_h[:N, :], side_h[N:, :])
    mine_g = jnp.where((b0 ^ b1) == 1, side_g, 0.0)
    out[:N, :] = jnp.where(a0 == 0, mine_h, mine_1)
    out[N : 2 * N, :] = jnp.where(a0 == 0, mine_1, mine_h)
    out[2 * N : 3 * N, :] = jnp.where(b0 == 0, mine_g, face0)
    out[3 * N :, :] = jnp.where(b0 == 0, face0, mine_g)


def call(body, outs, scratch, weight, *args):
    vmem = pl.BlockSpec(memory_space=pltpu.VMEM)
    return pl.pallas_call(
        body,
        out_shape=tuple(jax.ShapeDtypeStruct(shape, F32) for shape in outs),
        in_specs=[vmem] * len(args),
        out_specs=tuple(vmem for _ in outs),
        scratch_shapes=[pltpu.VMEM(shape, F32) for shape in scratch],
        compiler_params=pltpu.CompilerParams(vmem_limit_bytes=12 * 2**20),
        cost_estimate=pl.CostEstimate(flops=weight * 10**9, bytes_accessed=weight * 10**6, transcendentals=0),
    )(*args)


def flip(block, axis, bit):
    count = lax.axis_size(axis)
    return lax.ppermute(block, axis, [(i, i ^ (1 << bit)) for i in range(count)])


def tiles(count):
    return (count, N, N)


def shards(leaf_maps, leaf_fluxes):
    own_map, own_flux = leaf_maps[0, 0], leaf_fluxes[0, 0]
    mate_map = flip(own_map, "gy", 0)
    mate_flux = flip(own_flux, "gy", 0)
    map_v, flux_v = call(fetch, [(4 * N, 4 * N), (4 * N, N)], [], 1, own_map, own_flux)
    count = lax.axis_size("gx")
    inward = [pair for i in range(0, count, 4) for pair in ((i, i + 1), (i + 3, i + 2))]
    outward = [(b, a) for a, b in inward]
    inner = [pair for i in range(1, count, 4) for pair in ((i, i + 1), (i + 1, i))]
    square, wide = (N, N), (4 * N, 2 * N)

    x0, face, face_b = call(merge0, [square, tiles(1), tiles(2)], [square], 6, map_v, mate_map)
    got_a = lax.ppermute(face, "gx", inward)
    got_b = lax.ppermute(face_b, "gx", inward)
    sent1, flux1, kept1, y0, w0 = call(
        merge0_rest, [tiles(3), tiles(3), tiles(len(KEPT1)), (N, 5 * N), square], [(N, 6 * N), (5 * N, N)], 2,
        map_v, flux_v, mate_map, mate_flux, x0,
    )
    got_c = lax.ppermute(sent1, "gx", inward)
    got_d = lax.ppermute(flux1, "gx", inward)
    (xa,) = call(pair_0, [square], [square], 6, face, got_a)
    (x1,) = call(pair_1, [(2 * N, 2 * N)], [square, square], 6, xa, face_b, got_b)

    face, face_b = call(merge1, [tiles(1), tiles(2)], [(2 * N, 2 * N)], 1, x1, sent1, got_c)
    got_a = flip(face, "gy", 1)
    got_b = flip(face_b, "gy", 1)
    h2a, h2b, sent2, flux2, yt1, f1 = call(
        merge1_rest, [tiles(4), tiles(4), tiles(4), tiles(4), wide, (2 * N, N)], [wide], 2,
        x1, sent1, flux1, kept1, got_c, got_d,
    )
    got_c = flip(sent2, "gy", 1)
    (xa,) = call(pair_0, [square], [square], 6, face, got_a)
    got_e = flip(flux2, "gy", 1)
    (x2,) = call(pair_1, [(2 * N, 2 * N)], [square, square], 6, xa, face_b, got_b)
    got_d = flip(got_c, "gy", 0)

    low3, rows3, yt2 = call(merge2, [tiles(3), tiles(7), wide], [wide], 2, x2, h2a, h2b, got_c, got_d)
    got_a = lax.ppermute(low3, "gx", inner)
    _, flux3, sent3, own2, own1 = call(
        merge2_flux, [(2 * N, N), tiles(4), tiles(7), (2 * N, N), (2 * N, N)], [], 1,
        x2, x1, f1, yt2, flux2, got_e, rows3,
    )
    got_b = lax.ppermute(sent3, "gx", inner)
    z0, z1, s10, low10 = call(solve_low, [square] * 4, [square, tiles(2)], 12, low3, got_a)
    got_c = flip(got_b, "gy", 0)
    s20, l20, s21, l21, z2 = call(solve_2, [square] * 5, [square], 7, z0, z1, s10, rows3, got_b)
    kept, send = call(
        solve_3, [(5 * N, N), (3 * N, N)], [square, square, (4 * N, N), (4 * N, N)], 10,
        z0, z1, z2, s10, low10, s20, l20, s21, l21, rows3, flux3, got_b, got_c, yt2, own2, yt1, own1,
    )
    down = lax.ppermute(send, "gx", outward)
    (out,) = call(descend, [(4 * N, N)], [], 1, kept, down, y0, w0)
    return out[None, None]


def solution(mesh):
    spec = P("gx", "gy", None, None)

    return jax.shard_map(shards, mesh=mesh, in_specs=(spec, spec), out_specs=spec, check_vma=False)
```

```python
import jax
import jax.numpy as jnp
from jax import lax
from jax.experimental import pallas as pl
from jax.experimental.pallas import tpu as pltpu
from jax.sharding import PartitionSpec as P


N = 128
F32 = jnp.float32

SENT1 = ((4, 0), (4, 1), (4, 4))
FLUX1 = ((0, -1), (1, -1), (4, -1))
KEPT1 = ((2, 0), (2, 1), (3, 0), (3, 1), (2, 2), (3, 2), (3, 3), (2, 4), (3, 4), (2, -1), (3, -1))
HALF2 = (((2, 0), (2, 1), (3, 0), (3, 1)), ((2, 2), (3, 2), (3, 3)))
FLUX2 = ((0, -1), (1, -1), (2, -1), (3, -1))
SENT3 = (((0, 0), (1, 0), (1, 1)),)
ROWS3 = ((2, 0), (2, 1), (2, 2), (3, 0), (3, 1), (3, 2), (3, 3))


def put(batches, refs):
    return {t: (ref, i) for batch, ref in zip(batches, refs) for i, t in enumerate(batch)}


def roles():
    col = lax.axis_index("gx")
    row = lax.axis_index("gy")
    return col & 1, (col >> 1) & 1, row & 1, (row >> 1) & 1


def halves(x):
    top = x.astype(jnp.bfloat16)
    return top, (x - top.astype(F32)).astype(jnp.bfloat16)


def triple(x, y, dims):
    xh, xl = halves(x)
    yh, yl = halves(y)

    def dot(p, q):
        return lax.dot_general(p, q, (dims, ((), ())), preferred_element_type=F32)

    return dot(xh, yh) + (dot(xh, yl) + dot(xl, yh))


def mm(x, y):
    return triple(x, y, ((1,), (0,)))


def mm_nt(x, y):
    return triple(x, y, ((1,), (1,)))


def mm_tn(x, y):
    return triple(x, y, ((0,), (0,)))


def over(x, rows=8):
    return jnp.broadcast_to(x, (rows, N))


def invert(x_ref, v_ref):
    lane = lax.broadcasted_iota(jnp.int32, (8, N), 1)
    sub = lax.broadcasted_iota(jnp.int32, (8, N), 0)
    rows = [x_ref[8 * i : 8 * i + 8, :] for i in range(N // 8)]
    for j in range(N // 8):
        top = rows[j]
        inside = (lane >= 8 * j) & (lane < 8 * j + 8)
        seed = jnp.where(inside, jnp.where(lane - 8 * j == sub, 1.0, 0.0), top)
        cols = {c: over(top[:, 8 * j + c : 8 * j + c + 1]) for c in range(8)}
        panel = seed
        for k in range(0, 8, 2):
            a, b = over(cols[k][k : k + 1, :]), over(cols[k + 1][k : k + 1, :])
            d = over(cols[k + 1][k + 1 : k + 2, :])
            recip = 1.0 / (a * d - b * b)

            def pivot(x, k=k, cols=cols, a=a, b=b, d=d, recip=recip):
                t0, t1 = over(x[k : k + 1, :]), over(x[k + 1 : k + 2, :])
                s0, s1 = d * t0 - b * t1, a * t1 - b * t0
                pure = x - (cols[k] * s0 + cols[k + 1] * s1) * recip
                return jnp.where(sub == k, s0 * recip, jnp.where(sub == k + 1, s1 * recip, pure))

            panel = pivot(panel)
            cols = {c: pivot(cols[c]) for c in range(k + 2, 8)}
        low = lane < 8 * j + 8
        v_ref[8 * j : 8 * j + 8, :] = jnp.where(low, seed, 0.0)
        x_ref[8 * j : 8 * j + 8, :] = jnp.where(low, panel, 0.0)
        lines = [over(panel[k : k + 1, :]) for k in range(8)]
        for i in range(j + 1, N // 8):
            b = [over(rows[i][:, 8 * j + k : 8 * j + k + 1]) * lines[k] for k in range(8)]
            total = ((b[0] + b[1]) + (b[2] + b[3])) + ((b[4] + b[5]) + (b[6] + b[7]))
            rows[i] = jnp.where(inside, 0.0, rows[i]) - total
    x_ref[...] = mm_tn(v_ref[...], x_ref[...])


class Leaves:
    def __init__(self, own_map, mate_map, own_flux=None, mate_flux=None):
        a0, _, b0, b1 = roles()
        self.maps, self.fluxes = (own_map, mate_map), (own_flux, mate_flux)
        self.mine_low, self.g_up = b0 == 0, b1 == 0
        self.f1, self.h = 1 - a0, a0

    def pick(self, leaf, mine, mate):
        return jnp.where(self.mine_low, mine, mate) if leaf == 0 else jnp.where(self.mine_low, mate, mine)

    def entry(self, leaf, r, c):
        return self.pick(leaf, *(ref[at(r), at(c)] for ref in self.maps))

    def flux(self, leaf, r):
        return self.pick(leaf, *(ref[at(r), :] for ref in self.fluxes))


def at(side):
    return pl.ds(side * N, N) if isinstance(side, int) else pl.ds(pl.multiple_of(side * N, N), N)


def fetch(own_map, own_flux, map_out, flux_out):
    map_out[...] = own_map[...]
    flux_out[...] = own_flux[...]


def merge0(map_out, mate_map, x_ref, face0, face1, v_ref):
    a0, _, b0, _ = roles()
    low = b0 == 0
    f1, mine, his = 1 - a0, 3 - b0, 2 + b0
    x_ref[...] = map_out[at(mine), at(mine)] + mate_map[at(his), at(his)]
    invert(x_ref, v_ref)
    ours = (map_out[at(mine), at(f1)], map_out[at(f1), at(mine)], map_out[at(f1), at(f1)])
    theirs = (mate_map[at(his), at(f1)], mate_map[at(f1), at(his)], mate_map[at(f1), at(f1)])
    lower = [jnp.where(low, o, t) for o, t in zip(ours, theirs)]
    upper = [jnp.where(low, t, o) for o, t in zip(ours, theirs)]
    y_low, y_up = mm(x_ref[...], lower[0]), mm(x_ref[...], upper[0])
    face0[0] = lower[2] - mm(lower[1], y_low)
    face1[0] = -mm(upper[1], y_low)
    face1[1] = upper[2] - mm(upper[1], y_up)


def merge0_rest(own_map, own_flux, mate_map, mate_flux, x_ref, sent, flux_sent, kept, y_ref, w_ref, rhs, rows):
    leaves = Leaves(own_map, mate_map, own_flux, mate_flux)
    entry, flux, g_up = leaves.entry, leaves.flux, leaves.g_up
    face, other = (3, 2), (2, 3)
    owner = (0, 1, 0, 1)
    side = (leaves.f1, leaves.f1, leaves.h, leaves.h)
    for p in range(4):
        rhs[:, p * N : (p + 1) * N] = entry(owner[p], face[owner[p]], side[p])
        rows[p * N : (p + 1) * N, :] = entry(owner[p], side[p], face[owner[p]])
    rhs[:, 4 * N : 5 * N] = jnp.where(g_up, entry(1, 2, 3), entry(0, 3, 2))
    rows[4 * N : 5 * N, :] = jnp.where(g_up, entry(1, 3, 2), entry(0, 2, 3))
    rhs[:, 5 * N : 6 * N] = flux(0, 3) + flux(1, 2)
    out = mm(x_ref[...], rhs[...])
    y_ref[...] = out[:, : 5 * N]
    w_ref[...] = out[:, 5 * N :]
    home = put((SENT1, FLUX1, KEPT1), (sent, flux_sent, kept))
    for q, low, high in ((0, 2, 5), (1, 2, 5), (2, 2, 4), (3, 3, 4), (4, 2, 5), (-1, 0, 5)):
        cq = 5 if q < 0 else q
        drop = mm(rows[low * N : high * N, :], out[:, cq * N : (cq + 1) * N])
        for p in range(low, high):
            value = -drop[(p - low) * N : (p - low + 1) * N, :]
            if q < 0:
                if p < 4:
                    value = value + flux(owner[p], side[p])
                else:
                    value = value + jnp.where(g_up, flux(1, 3), flux(0, 2))
            elif p < 4 and q < 4:
                if owner[p] == owner[q]:
                    value = value + entry(owner[p], side[p], side[q])
            elif p < 4:
                part = entry(owner[p], side[p], other[owner[p]])
                value = value + jnp.where(g_up if owner[p] == 1 else jnp.logical_not(g_up), part, 0.0)
            elif q < 4:
                part = entry(owner[q], other[owner[q]], side[q])
                value = value + jnp.where(g_up if owner[q] == 1 else jnp.logical_not(g_up), part, 0.0)
            else:
                value = value + jnp.where(g_up, entry(1, 3, 3), entry(0, 2, 2))
            ref, i = home[(p, q)]
            ref[i] = value


def pair_0(own, got, x_out, v_ref):
    x_out[...] = own[0] + got[0]
    invert(x_out, v_ref)


def pair_1(x11, own, got, x_out, x22, v_ref):
    s = own[0] + got[0]
    t = mm(s, x11[...])
    x22[...] = own[1] + got[1] - mm_nt(t, s)
    invert(x22, v_ref)
    low = mm(x22[...], t)
    x_out[N:, N:] = x22[...]
    x_out[N:, :N] = -low
    x_out[:N, N:] = -mm_tn(t, x22[...])
    x_out[:N, :N] = x11[...] + mm_tn(t, low)


def load(table, t):
    ref, i = table[t]
    return ref[i]


def merge1(x, own, got, face0, face1, a_ref):
    for q in range(2):
        cols = slice(q * N, (q + 1) * N)
        a_ref[0:N, cols] = own[q]
        a_ref[N:, cols] = got[q]
    yt = mm(a_ref[...], x[...])
    drop = mm_nt(yt, a_ref[0:N, :])
    face0[0] = own[2] - drop[:N]
    face1[0] = -drop[N:]
    face1[1] = got[2] - mm_nt(yt[N:], a_ref[N:, :])


def merge1_rest(x, own, own_flux, kept, got, got_flux, half0, half1, send, flux2, yt_ref, f_ref, a_ref):
    core = roles()[2]
    mine = put((SENT1, FLUX1, KEPT1), (own, own_flux, kept))
    theirs = put((SENT1, FLUX1), (got, got_flux))
    for q in range(2):
        cols = slice(q * N, (q + 1) * N)
        a_ref[0:N, cols] = load(mine, (4, q))
        a_ref[N : 2 * N, cols] = load(theirs, (4, q))
        a_ref[2 * N : 3 * N, cols] = load(mine, (2, q))
        a_ref[3 * N : 4 * N, cols] = load(mine, (3, q))
        f_ref[cols, :] = load(mine, (q, -1)) + load(theirs, (q, -1))
    yt_ref[...] = mm(a_ref[...], x[...])
    base = {
        (2, 0): (mine, (2, 4)), (3, 0): (mine, (3, 4)),
        (2, 2): (mine, (2, 2)), (3, 2): (mine, (3, 2)), (3, 3): (mine, (3, 3)),
        (0, -1): (mine, (4, -1)), (1, -1): (theirs, (4, -1)), (2, -1): (mine, (2, -1)), (3, -1): (mine, (3, -1)),
    }
    spread(((0, 2), (1, 2), (2, 2), (3, 3), (-1, 0)), HALF2 + (FLUX2,), (half0, half1, flux2), base, load, yt_ref, a_ref, f_ref)
    half1[3] = jnp.zeros((N, N), F32)
    pick_half(core, half0, half1, send)


def spread(spans, batches, refs, base, take, yt, a_ref, f_ref):
    for q, low in spans:
        if q < 0:
            drop = mm(yt[...], f_ref[...])
        else:
            drop = mm_nt(yt[low * N :, :], a_ref[q * N : (q + 1) * N, :])
        for p in range(low, 4):
            value = -drop[(p - low) * N : (p - low + 1) * N, :]
            if (p, q) in base:
                value = value + take(*base[(p, q)])
            for batch, ref in zip(batches, refs):
                if (p, q) in batch:
                    ref[batch.index((p, q))] = value


def pick_half(core, half0, half1, send):
    @pl.when(core == 0)
    def _():
        send[...] = half0[...]

    @pl.when(core == 1)
    def _():
        send[...] = half1[...]


def sides2(half0, half1, got, swapped):
    core, b1 = roles()[2:]
    table = put(HALF2, (half0, half1))
    which = {t: h for h in range(2) for t in HALF2[h]}

    def mate(t):
        i = table[t][1]
        return jnp.where(core == which[t], got[i], swapped[i])

    def of(half, t):
        return jnp.where(b1 == half, load(table, t), mate(t))

    return of


def merge2(x, half0, half1, got, swapped, sent0, rows3, yt_ref, a_ref):
    of = sides2(half0, half1, got, swapped)
    for q in range(2):
        for p in range(4):
            a_ref[p * N : (p + 1) * N, q * N : (q + 1) * N] = of(p // 2, (2 + p % 2, q))
    yt_ref[...] = mm(a_ref[...], x[...])
    base = {(p, q): (p // 2, (2 + p % 2, 2 + q % 2)) for p in range(4) for q in range(p + 1) if p // 2 == q // 2}
    spans = ((0, 0), (1, 1), (2, 2), (3, 3))
    spread(spans, SENT3 + (ROWS3,), (sent0, rows3), base, of, yt_ref, a_ref, None)


def merge2_flux(yt2, own, got, rows3, f2, flux3, send):
    core, b1 = roles()[2:]
    f2[:N, :] = own[0] + got[0]
    f2[N:, :] = own[1] + got[1]
    drop = mm(yt2[...], f2[...])
    for p in range(4):
        value = jnp.where(b1 == p // 2, own[2 + p % 2], got[2 + p % 2])
        flux3[p] = value - drop[p * N : (p + 1) * N]
    send[:3] = rows3[:3]

    @pl.when(core == 0)
    def _():
        send[3:] = rows3[3:]

    @pl.when(core == 1)
    def _():
        send[3:] = flux3[...]


def own_parts(x2, f2, x1, f1, own2, own1):
    own2[...] = mm(x2[...], f2[...])
    own1[...] = mm(x1[...], f1[...])


def solve_low(own, got, x0, x1, s10, low10, v_ref, xs):
    xs[0] = own[0] + got[0]
    s10[...] = own[1] + got[1]
    xs[1] = own[2] + got[2]

    def step(i, carry):
        invert(xs.at[i], v_ref)

        @pl.when(i == 0)
        def _():
            low10[...] = mm(s10[...], xs[0])
            xs[1] = xs[1] - mm_nt(low10[...], s10[...])

        return carry

    lax.fori_loop(0, 2, step, 0)
    x0[...] = xs[0]
    x1[...] = xs[1]


def solve_2(x0, x1, s10, half3, got, s20, l20, s21, l21, x_out, v_ref):
    s = half3[0] + got[0]
    low = mm(s, x0[...])
    s20[...], l20[...] = s, low
    t = half3[1] + got[1] - mm_nt(low, s10[...])
    u = mm(t, x1[...])
    s21[...], l21[...] = t, u
    x_out[...] = half3[2] + got[2] - mm_nt(low, s) - mm_nt(u, t)
    invert(x_out, v_ref)


def solve_3(x0, x1, x2, s10, low10, s20, l20, s21, l21, rows3, flux3, got, swapped, yt2, own2, yt1, own1,
            kept, send, x3, v_ref, u, v):
    _, _, core, b1 = roles()

    def mate(h, i):
        return jnp.where(core == h, got[i], swapped[i])

    s30 = rows3[3] + mate(0, 3)
    l30 = mm(s30, x0[...])
    s31 = rows3[4] + mate(0, 4) - mm_nt(l30, s10[...])
    l31 = mm(s31, x1[...])
    s32 = rows3[5] + mate(0, 5) - mm_nt(l30, s20[...]) - mm_nt(l31, s21[...])
    l32 = mm(s32, x2[...])
    x3[...] = rows3[6] + mate(0, 6) - mm_nt(l30, s30) - mm_nt(l31, s31) - mm_nt(l32, s32)
    invert(x3, v_ref)
    f = [flux3[i] + mate(1, 3 + i) for i in range(4)]
    f[1] = f[1] - mm(low10[...], f[0])
    f[2] = f[2] - mm(l20[...], f[0]) - mm(l21[...], f[1])
    f[3] = f[3] - mm(l30, f[0]) - mm(l31, f[1]) - mm(l32, f[2])
    p2, p1, p0 = mm(x2[...], f[2]), mm(x1[...], f[1]), mm(x0[...], f[0])
    w3 = mm(x3[...], f[3])
    w2 = p2 - mm_tn(l32, w3)
    w1 = p1 - mm_tn(l31, w3) - mm_tn(l21[...], w2)
    w0 = p0 - mm_tn(l30, w3) - mm_tn(l20[...], w2) - mm_tn(low10[...], w1)
    for i, w in enumerate((w0, w1, w2, w3)):
        u[i * N : (i + 1) * N, :] = -w
    face2 = -(mm_tn(yt2[...], u[...]) + own2[...])
    v[: 2 * N, :] = face2
    v[2 * N :, :] = jnp.where(b1 == 0, u[: 2 * N, :], u[2 * N :, :])
    face1 = -(mm_tn(yt1[...], v[...]) + own1[...])
    kept[: 2 * N, :] = face1
    kept[2 * N : 4 * N, :] = v[2 * N :, :]
    kept[4 * N :, :] = face2[:N, :]
    send[: 2 * N, :] = face1
    send[2 * N :, :] = face2[N:, :]


def descend(kept, got, y0, w0, out):
    a0, a1, b0, b1 = roles()
    inner = (a0 ^ a1) == 1
    face1 = jnp.where(inner, kept[: 2 * N, :], got[: 2 * N, :])
    side_h = jnp.where(inner, kept[2 * N : 4 * N, :], 0.0)
    side_g = jnp.where(inner, kept[4 * N :, :], got[2 * N :, :])
    face0 = -(mm(y0[...], jnp.concatenate([face1, side_h, side_g], axis=0)) + w0[...])
    mine_1 = jnp.where(b0 == 0, face1[:N, :], face1[N:, :])
    mine_h = jnp.where(b0 == 0, side_h[:N, :], side_h[N:, :])
    mine_g = jnp.where((b0 ^ b1) == 1, side_g, 0.0)
    out[:N, :] = jnp.where(a0 == 0, mine_h, mine_1)
    out[N : 2 * N, :] = jnp.where(a0 == 0, mine_1, mine_h)
    out[2 * N : 3 * N, :] = jnp.where(b0 == 0, mine_g, face0)
    out[3 * N :, :] = jnp.where(b0 == 0, face0, mine_g)


def call(body, outs, scratch, weight, *args):
    vmem = pl.BlockSpec(memory_space=pltpu.VMEM)
    return pl.pallas_call(
        body,
        out_shape=tuple(jax.ShapeDtypeStruct(shape, F32) for shape in outs),
        in_specs=[vmem] * len(args),
        out_specs=tuple(vmem for _ in outs),
        scratch_shapes=[pltpu.VMEM(shape, F32) for shape in scratch],
        compiler_params=pltpu.CompilerParams(vmem_limit_bytes=12 * 2**20),
        cost_estimate=pl.CostEstimate(flops=weight * 10**9, bytes_accessed=weight * 10**6, transcendentals=0),
    )(*args)


def flip(block, axis, bit):
    count = lax.axis_size(axis)
    return lax.ppermute(block, axis, [(i, i ^ (1 << bit)) for i in range(count)])


def tiles(count):
    return (count, N, N)


def shards(leaf_maps, leaf_fluxes):
    own_map, own_flux = leaf_maps[0, 0], leaf_fluxes[0, 0]
    mate_map = flip(own_map, "gy", 0)
    mate_flux = flip(own_flux, "gy", 0)
    map_v, flux_v = call(fetch, [(4 * N, 4 * N), (4 * N, N)], [], 1, own_map, own_flux)
    count = lax.axis_size("gx")
    inward = [pair for i in range(0, count, 4) for pair in ((i, i + 1), (i + 3, i + 2))]
    outward = [(b, a) for a, b in inward]
    inner = [pair for i in range(1, count, 4) for pair in ((i, i + 1), (i + 1, i))]
    square, wide = (N, N), (4 * N, 2 * N)

    x0, face, face_b = call(merge0, [square, tiles(1), tiles(2)], [square], 6, map_v, mate_map)
    got_a = lax.ppermute(face, "gx", inward)
    got_b = lax.ppermute(face_b, "gx", inward)
    sent1, flux1, kept1, y0, w0 = call(
        merge0_rest, [tiles(3), tiles(3), tiles(len(KEPT1)), (N, 5 * N), square], [(N, 6 * N), (5 * N, N)], 2,
        map_v, flux_v, mate_map, mate_flux, x0,
    )
    got_c = lax.ppermute(sent1, "gx", inward)
    got_d = lax.ppermute(flux1, "gx", inward)
    (xa,) = call(pair_0, [square], [square], 6, face, got_a)
    (x1,) = call(pair_1, [(2 * N, 2 * N)], [square, square], 6, xa, face_b, got_b)

    face, face_b = call(merge1, [tiles(1), tiles(2)], [(2 * N, 2 * N)], 1, x1, sent1, got_c)
    got_a = flip(face, "gy", 1)
    got_b = flip(face_b, "gy", 1)
    h2a, h2b, sent2, flux2, yt1, f1 = call(
        merge1_rest, [tiles(4), tiles(4), tiles(4), tiles(4), wide, (2 * N, N)], [wide], 2,
        x1, sent1, flux1, kept1, got_c, got_d,
    )
    got_c = flip(sent2, "gy", 1)
    (xa,) = call(pair_0, [square], [square], 6, face, got_a)
    got_e = flip(flux2, "gy", 1)
    (x2,) = call(pair_1, [(2 * N, 2 * N)], [square, square], 6, xa, face_b, got_b)
    got_d = flip(got_c, "gy", 0)

    low3, rows3, yt2 = call(merge2, [tiles(3), tiles(7), wide], [wide], 2, x2, h2a, h2b, got_c, got_d)
    got_a = lax.ppermute(low3, "gx", inner)
    f2, flux3, sent3 = call(merge2_flux, [(2 * N, N), tiles(4), tiles(7)], [], 1, yt2, flux2, got_e, rows3)
    own2, own1 = call(own_parts, [(2 * N, N), (2 * N, N)], [], 1, x2, f2, x1, f1)
    got_b = lax.ppermute(sent3, "gx", inner)
    z0, z1, s10, low10 = call(solve_low, [square] * 4, [square, tiles(2)], 12, low3, got_a)
    got_c = flip(got_b, "gy", 0)
    s20, l20, s21, l21, z2 = call(solve_2, [square] * 5, [square], 7, z0, z1, s10, rows3, got_b)
    kept, send = call(
        solve_3, [(5 * N, N), (3 * N, N)], [square, square, (4 * N, N), (4 * N, N)], 10,
        z0, z1, z2, s10, low10, s20, l20, s21, l21, rows3, flux3, got_b, got_c, yt2, own2, yt1, own1,
    )
    down = lax.ppermute(send, "gx", outward)
    (out,) = call(descend, [(4 * N, N)], [], 1, kept, down, y0, w0)
    return out[None, None]


def solution(mesh):
    spec = P("gx", "gy", None, None)

    return jax.shard_map(shards, mesh=mesh, in_specs=(spec, spec), out_specs=spec, check_vma=False)
```
